512 devices in a mesh: sx: 8 (over z), sy: 8 (over y), cg: 8 (over x, core).
Axes of the slice: x: 4, y: 8, z: 8, core: 2. Of those that a mesh axis runs over, the one named last changes fastest.
Arguments:
- right_side: float32 [512, 1024, 128], P(('sx', 'cg'), 'sy'), may hold values from -6 to 18, as said below
- perm_class: int32 [512, 1024, 128], P(('sx', 'cg'), 'sy'), may hold values from 0 to 15
- perm_table: float32 [2, 16], replicated, may hold values from 0.02 to 2
Outputs:
- solution: float32 [512, 1024, 128], P(('sx', 'cg'), 'sy')
- residual: float32 [512, 1024, 128], P(('sx', 'cg'), 'sy')
The draws below stay inside these ranges and needn't reach their ends.
Inputs may be any that keep to these rules, and one draw needn't show every extreme that they name: `right_side`: source terms, one real value a cell.
All inputs are finite; a program needn't handle non-finite values.
Results may differ from the reference program's by a relative error of at most 0.0003.
Values sent between devices are 32-bit elements; how exact they have to be, the bound alone decides.
No kernel may reach another device: no remote copies, remote signals or barrier semaphores. Data moves between devices by JAX's collectives and lax.ppermute only.
A program may use at most 64 MiB of HBM per device.

```python
import math
import jax
import jax.numpy as jnp
from jax import lax

NZ = 128
AZ = 4
NCLASS = 16
ITERS = 2
COARSE_ITERS = 4
NX = 512
NY = 1024
MX = 256
MY = 32


def draw_right_side(key, part):
    extent = (NX, NY, NZ)
    along_x = lax.broadcasted_iota(jnp.float32, extent, 0) / (NX - 1)
    noise = jnp.clip(jax.random.normal(key, extent, jnp.float32), -3.0, 3.0)
    return (1.0 + 2.0 * along_x) * (1.0 + noise)


def touch_ends(values, stream_key, smallest, top_value):
    spot = [jax.random.randint(jax.random.fold_in(stream_key, axis), (), 0, length) for axis, length in enumerate(values.shape)]
    widest = values.shape.index(max(values.shape))
    neighbour = spot[:widest] + [(spot[widest] + 1) % values.shape[widest]] + spot[widest + 1:]
    return values.at[tuple(spot)].set(smallest).at[tuple(neighbour)].set(top_value)


def setup_inputs(seed: int = 0) -> dict:
    splits = jax.random.split(jax.random.key(seed), 4)
    right_side = draw_right_side(jax.random.fold_in(splits[3], 71), 0)
    perm_class = touch_ends(jax.random.randint(splits[1], (NX, NY, NZ), 0, NCLASS), jax.random.fold_in(splits[1], 1), 0, NCLASS - 1).astype(jnp.int32)
    perm_table = jnp.clip(jnp.exp(jax.random.uniform(splits[2], (2, NCLASS), jnp.float32, math.log(0.02), math.log(2.0))), 0.02, 2.0)
    return dict(right_side=right_side, perm_class=perm_class, perm_table=perm_table)


omega_fine = 2.0 / 3.0
omega_coarse = 2.0 / 3.0


def lower_shift(values):
    zero_col = jnp.zeros_like(values[..., :1])
    return jnp.concatenate([zero_col, values[..., :-1]], axis=-1)


def upper_shift(values):
    zero_col = jnp.zeros_like(values[..., :1])
    return jnp.concatenate([values[..., 1:], zero_col], axis=-1)


def harmonic(left, right):
    return 2.0 * left * right / (left + right)


def apply_rimmed(coefs, values, rimmed):
    x_low, x_high, y_low, y_high, z_up, centre = coefs
    beside = x_low * rimmed[:-2, 1:-1] + x_high * rimmed[2:, 1:-1]
    beside = beside + y_low * rimmed[1:-1, :-2] + y_high * rimmed[1:-1, 2:]
    beside = beside + z_up * upper_shift(values) + lower_shift(z_up * values)
    return centre * values - beside


def padded(values):
    return jnp.pad(values, ((1, 1), (1, 1), (0, 0)))


def apply_whole(coefs, values):
    return apply_rimmed(coefs, values, padded(values))


def block_sum(values, extent):
    count_x, count_y, count_z = extent
    size_x, size_y, size_z = values.shape
    blocks = values.reshape(count_x, size_x // count_x, count_y, size_y // count_y, count_z, size_z // count_z)
    return blocks.sum(axis=(1, 3, 5))


def coarse_coefs(fine, extent):
    x_low, x_high, y_low, y_high, z_up, centre = fine
    span_x = x_low.shape[0] // extent[0]
    span_y = x_low.shape[1] // extent[1]
    span_z = x_low.shape[2] // extent[2]
    pieces = [
        block_sum(x_low[0::span_x], extent),
        block_sum(x_high[span_x - 1::span_x], extent),
        block_sum(y_low[:, 0::span_y], extent),
        block_sum(y_high[:, span_y - 1::span_y], extent),
        block_sum(z_up[:, :, span_z - 1::span_z], extent),
    ]
    summed = pieces[0] + pieces[1] + pieces[2] + pieces[3] + pieces[4] + lower_shift(pieces[4])
    return jnp.stack(pieces + [summed])


def prolong(values, extent):
    count_x, count_y, count_z = values.shape
    size_x, size_y, size_z = extent
    spread = jnp.broadcast_to(values[:, None, :, None, :, None], (count_x, size_x // count_x, count_y, size_y // count_y, count_z, size_z // count_z))
    return spread.reshape(extent)


def coarse_solve(coarse, source):
    centre = coarse[5]
    values = omega_coarse * source / centre
    for sweep in range(COARSE_ITERS - 1):
        values = values + omega_coarse * (source - apply_whole(tuple(coarse), values)) / centre
    return values


def precondition(fine, coarse, residual):
    centre = fine[5]
    sweep_one = omega_fine * residual / centre
    smooth = sweep_one + omega_fine * (residual - apply_whole(fine, sweep_one)) / centre
    correction = coarse_solve(coarse, block_sum(residual, coarse.shape[1:]))
    return smooth + prolong(correction, residual.shape)


def reference(right_side, perm_class, perm_table):
    horizontal = jnp.zeros(perm_class.shape, jnp.float32)
    vertical = jnp.zeros(perm_class.shape, jnp.float32)
    for category in range(NCLASS):
        matches = perm_class == category
        horizontal = jnp.where(matches, perm_table[0, category], horizontal)
        vertical = jnp.where(matches, perm_table[1, category], vertical)
    rimmed = padded(horizontal)
    x_faces = harmonic(rimmed[:-1, 1:-1], rimmed[1:, 1:-1])
    x_low = x_faces[:-1].at[0].set(2.0 * horizontal[0])
    x_high = x_faces[1:].at[-1].set(2.0 * horizontal[-1])
    y_faces = harmonic(rimmed[1:-1, :-1], rimmed[1:-1, 1:])
    y_low = y_faces[:, :-1].at[:, 0].set(2.0 * horizontal[:, 0])
    y_high = y_faces[:, 1:].at[:, -1].set(2.0 * horizontal[:, -1])
    z_up = harmonic(vertical, upper_shift(vertical))
    centre = x_low + x_high + y_low + y_high + z_up + lower_shift(z_up)
    fine = (x_low, x_high, y_low, y_high, z_up, centre)
    coarse = coarse_coefs(fine, (MX, MY, AZ))
    solution = jnp.zeros_like(right_side)
    residual = right_side
    direction = precondition(fine, coarse, residual)
    fit_now = jnp.sum(residual * direction)
    for iteration in range(ITERS):
        applied = apply_whole(fine, direction)
        step_size = fit_now / jnp.sum(direction * applied)
        solution = solution + step_size * direction
        residual = residual - step_size * applied
        if iteration + 1 < ITERS:
            smoothed = precondition(fine, coarse, residual)
            fit_next = jnp.sum(residual * smoothed)
            direction = smoothed + (fit_next / fit_now) * direction
            fit_now = fit_next
    return solution, residual
```

```python
import jax
import jax.numpy as jnp
from jax import lax
from jax.experimental import pallas as pl
from jax.experimental.pallas import tpu as pltpu
from jax.sharding import PartitionSpec as P

F32 = jnp.float32
W = 2.0 / 3.0
X_AXES = ("sx", "cg")
SWEEPS = 3

NXL, NYL, NZ = 8, 128, 128
HX = 3
PLANES = NXL + 2 * HX
ROWS = 160
OWN = 16
CHUNKS = ((8, 8, -1), (16, 32, 0), (48, 32, 1), (80, 32, 2), (112, 32, 3), (144, 8, 4))
OWN_CHUNKS = CHUNKS[1:5]
X_LOW, X_HIGH, Y_LOW, Y_HIGH, Z_UP, SOURCE = range(6)


def harmonic(a, b):
    return 2.0 * a * b / (a + b)


def up(v):
    return pltpu.roll(v, NZ - 1, 1)


def down(v):
    return pltpu.roll(v, 1, 1)


def look_up(row, index):
    table = jnp.broadcast_to(row, index.shape)
    return jnp.take_along_axis(table, index, axis=1, mode="promise_in_bounds")


def iota(shape, dim):
    return lax.broadcasted_iota(jnp.int32, shape, dim)


def dot(a, b):
    return jnp.dot(a, b, precision=lax.Precision.HIGHEST, preferred_element_type=F32)


def sum_matrix():
    return jnp.where(iota((NZ, NZ), 0) // 32 == iota((NZ, NZ), 1) % 4, 1.0, 0.0).astype(F32)


def top_matrix():
    lane, col = iota((NZ, NZ), 0), iota((NZ, NZ), 1) % 4
    return jnp.where((lane == 32 * col + 31) & (col < 3), 1.0, 0.0).astype(F32)


def row_group(values):
    return (values[0:8] + values[8:16]) + (values[16:24] + values[24:32])


def gather_tile(pieces):
    group = iota((8, NZ), 1) // 4
    sublane = iota((8, NZ), 0)
    tile = jnp.zeros((8, NZ), F32)
    for a, parts in enumerate(pieces):
        acc = jnp.zeros((8, NZ), F32)
        for field, j, part in parts:
            acc = jnp.where(group == 4 * field + j, part, acc)
        tile = jnp.where(sublane == a, jnp.sum(acc, axis=0, keepdims=True), tile)
    return tile


def coarse_kernel(
    inside, table, cls, rhs, xlo, xhi, ylo, yhi, out, kh, tiles, ztiles
):
    khrow, kvrow = table[0:1, :], table[1:2, :]

    def own(x, _):
        index = cls[x]
        kh[x + 1, 8:136, :] = look_up(khrow, index)
        kh[x + 1, 0:8, :] = look_up(khrow, ylo[x].astype(jnp.int32))
        kh[x + 1, 136:144, :] = look_up(khrow, yhi[x].astype(jnp.int32))
        return 0

    lax.fori_loop(0, NXL, own, 0)
    kh[0, 8:136, :] = look_up(khrow, xlo[2].astype(jnp.int32))
    kh[NXL + 1, 8:136, :] = look_up(khrow, xhi[0].astype(jnp.int32))

    first = iota((8, NZ), 0) == 0
    for f in range(5):
        for j in range(4):
            rows = pl.ds(8 + 32 * j, 32)
            low, high = kh[2 * f, rows, :], kh[2 * f + 1, rows, :]
            face = harmonic(low, high)
            if f == 0:
                face = jnp.where(inside[0] > 0.5, face, 2.0 * high)
            if f == 4:
                face = jnp.where(inside[1] > 0.5, face, 2.0 * low)
            tiles[pl.ds(8 * (4 * f + j), 8), :] = row_group(face)
    for a in range(4):
        for j in range(5):
            total = jnp.zeros((8, NZ), F32)
            for x in (2 * a, 2 * a + 1):
                low = kh[x + 1, pl.ds(7 + 32 * j, 8), :]
                high = kh[x + 1, pl.ds(8 + 32 * j, 8), :]
                face = harmonic(low, high)
                if j == 0:
                    face = jnp.where(inside[2] > 0.5, face, 2.0 * high)
                if j == 4:
                    face = jnp.where(inside[3] > 0.5, face, 2.0 * low)
                total = total + face
            tiles[pl.ds(8 * (20 + 5 * a + j), 8), :] = jnp.where(first, total, 0.0)
        for j in range(4):
            rows = pl.ds(32 * j, 32)
            source = rhs[2 * a, rows, :] + rhs[2 * a + 1, rows, :]
            tiles[pl.ds(8 * (40 + 4 * a + j), 8), :] = row_group(source)
            kv0 = look_up(kvrow, cls[2 * a, rows, :])
            kv1 = look_up(kvrow, cls[2 * a + 1, rows, :])
            upper = harmonic(kv0, up(kv0)) + harmonic(kv1, up(kv1))
            ztiles[pl.ds(8 * (4 * a + j), 8), :] = row_group(upper)
    tiles[...] = dot(tiles[...], sum_matrix())
    ztiles[...] = dot(ztiles[...], top_matrix())

    def part(t):
        return tiles[pl.ds(8 * t, 8), :]

    pieces = []
    for a in range(4):
        parts = []
        for j in range(4):
            parts += [
                (X_LOW, j, part(4 * a + j)),
                (X_HIGH, j, part(4 * (a + 1) + j)),
                (Y_LOW, j, part(20 + 5 * a + j)),
                (Y_HIGH, j, part(20 + 5 * a + j + 1)),
                (Z_UP, j, ztiles[pl.ds(8 * (4 * a + j), 8), :]),
                (SOURCE, j, part(40 + 4 * a + j)),
            ]
        pieces.append(parts)
    out[...] = gather_tile(pieces)


def stack_tiles(buf, left, own, right):
    buf[0:4, :] = left[0:4, :]
    buf[4:8, :] = own[0:4, :]
    buf[8:12, :] = right[0:4, :]
    buf[12:16, :] = jnp.zeros((4, NZ), F32)
    return buf[...]


def widen(field, below, own, above):
    lane = iota((16, NZ), 1)

    def placed(v, at):
        shift = (at - 16 * field) % NZ
        return pltpu.roll(v, shift, 1) if shift else v

    wide = jnp.where(lane < 16, placed(below, 0), placed(own, 16))
    wide = jnp.where(lane < 32, wide, placed(above, 32))
    return jnp.where(lane < 48, wide, 0.0)


def coarse_sweeps(coefs, source):
    x_low, x_high, y_low, y_high, z_up, scale = coefs
    start = scale * source
    c = start
    for _ in range(SWEEPS):
        beside = x_low * pltpu.roll(c, 1, 0) + x_high * pltpu.roll(c, 15, 0)
        beside = beside + y_low * pltpu.roll(c, 4, 1) + y_high * pltpu.roll(c, NZ - 4, 1)
        beside = beside + z_up * up(c) + down(z_up * c)
        c = (1.0 - W) * c + (start + scale * beside)
    return c


def spread_coarse(c, spread):
    for k in range(6):
        lane = iota((NZ, NZ), 1)
        pick = jnp.where(iota((NZ, NZ), 0) == 4 * (k + 3) + lane // 32, 1.0, 0.0)
        spread[k] = dot(c, pick.astype(F32))


def neighbours(v, fx, fy, fz, i, at, size):
    here = v[i, pl.ds(at, size), :]
    total = fx[i, pl.ds(at, size), :] * v[i - 1, pl.ds(at, size), :]
    total = total + fx[i + 1, pl.ds(at, size), :] * v[i + 1, pl.ds(at, size), :]
    total = total + fy[i, pl.ds(at, size), :] * v[i, pl.ds(at - 1, size), :]
    total = total + fy[i, pl.ds(at + 1, size), :] * v[i, pl.ds(at + 1, size), :]
    z = fz[i, pl.ds(at, size), :]
    return here, total + z * up(here) + down(z * here)


def smooth(s1, d, fx, fy, fz, scale, spread):
    def plane(i, _):
        for at, size, j in CHUNKS:
            here, total = neighbours(s1, fx, fy, fz, i, at, size)
            value = (2.0 - W) * here + scale[i, pl.ds(at, size), :] * total
            d[i, pl.ds(at, size), :] = value + spread[j + 1, pl.ds((i + 5) // 2, 1), :]
        return 0

    lax.fori_loop(HX - 1, HX + NXL + 1, plane, 0)


def zero_pads(v):
    def plane(i, _):
        v[i, 0:8, :] = jnp.zeros((8, NZ), F32)
        v[i, ROWS - 8 : ROWS, :] = jnp.zeros((8, NZ), F32)
        return 0

    lax.fori_loop(0, PLANES, plane, 0)


def first_kernel(
    inside, table, cls, rhs, xlo, xhi, ylo, yhi, left, own, right, below, above,
    d_out, q_out, xm_lo, xm_hi, tile_out, coefs_out, fx, fy, fz, scale, centre,
    kh, kv, s1, d, stack, spread, tiles,
):
    khrow, kvrow = table[0:1, :], table[1:2, :]

    def put(i, at, size, classes, with_kv):
        index = classes.astype(jnp.int32)
        kh[i, pl.ds(at, size), :] = look_up(khrow, index)
        if with_kv:
            kv[i, pl.ds(at, size), :] = look_up(kvrow, index)

    def plane(x, _):
        i = x + HX
        put(i, OWN, NYL, cls[x], True)
        put(i, 8, 8, ylo[x], True)
        put(i, 144, 8, yhi[x], True)
        s1[i, 16:144, :] = rhs[x]
        s1[i, 8:16, :] = ylo[NXL + x]
        s1[i, 144:152, :] = yhi[NXL + x]
        return 0

    lax.fori_loop(0, NXL, plane, 0)
    for n in range(3):
        for base, msg, corner in ((0, xlo, 0), (HX + NXL, xhi, 3)):
            i = base + n
            with_kv = 0 < i < PLANES - 1
            put(i, OWN, NYL, msg[n], with_kv)
            put(i, 8, 8, below[corner + n], with_kv)
            put(i, 144, 8, above[corner + n], with_kv)
    for n in range(2):
        for i, msg, corner in ((1 + n, xlo, 6), (HX + NXL + n, xhi, 8)):
            s1[i, 16:144, :] = msg[3 + n]
            s1[i, 8:16, :] = below[corner + n]
            s1[i, 144:152, :] = above[corner + n]

    def pads(i, _):
        ones = jnp.ones((8, NZ), F32)
        kh[i, 0:8, :] = ones
        kh[i, ROWS - 8 : ROWS, :] = ones
        fy[i, ROWS - 8 : ROWS, :] = ones
        return 0

    lax.fori_loop(0, PLANES, pads, 0)
    zero_pads(s1)
    zero_pads(d)

    mid = stack_tiles(stack, left, own, right)
    low = stack_tiles(stack, below[10], below[11], below[12])
    high = stack_tiles(stack, above[10], above[11], above[12])
    wide = [widen(k, low, mid, high) for k in range(6)]
    total = wide[0] + wide[1] + wide[2] + wide[3] + wide[4] + down(wide[4])
    valid = total > 0.0
    wide_scale = jnp.where(valid, W / jnp.where(valid, total, 1.0), 0.0)
    coefs = wide[:5] + [wide_scale]
    for k in range(6):
        coefs_out[k] = coefs[k]
    spread_coarse(coarse_sweeps(coefs, wide[SOURCE]), spread)

    def faces(i, _):
        for at, size, _j in CHUNKS:
            rows = pl.ds(at, size)
            here = kh[i, rows, :]
            fx[i, rows, :] = harmonic(kh[i - 1, rows, :], here)
            fy[i, rows, :] = harmonic(kh[i, pl.ds(at - 1, size), :], here)
            k = kv[i, rows, :]
            z = harmonic(k, up(k))
            fz[i, rows, :] = jnp.where(iota((size, NZ), 1) < NZ - 1, z, 0.0)
        return 0

    lax.fori_loop(1, PLANES - 1, faces, 0)
    for at, size, _j in CHUNKS:
        rows = pl.ds(at, size)
        fx[PLANES - 1, rows, :] = harmonic(
            kh[PLANES - 2, rows, :], kh[PLANES - 1, rows, :]
        )

    @pl.when(inside[0] < 0.5)
    def _():
        fx[HX] = 2.0 * kh[HX]

    @pl.when(inside[1] < 0.5)
    def _():
        fx[HX + NXL] = 2.0 * kh[HX + NXL - 1]

    @pl.when(inside[2] < 0.5)
    def _():
        for i in range(1, PLANES - 1):
            fy[i, OWN : OWN + 1, :] = 2.0 * kh[i, OWN : OWN + 1, :]

    @pl.when(inside[3] < 0.5)
    def _():
        for i in range(1, PLANES - 1):
            fy[i, 144:145, :] = 2.0 * kh[i, 143:144, :]

    def scales(i, _):
        x_mask = jnp.where(i < HX, inside[0], jnp.where(i >= HX + NXL, inside[1], 1.0))
        for at, size, j in CHUNKS:
            rows, above_rows = pl.ds(at, size), pl.ds(at + 1, size)
            z = fz[i, rows, :]
            total = fx[i, rows, :] + fx[i + 1, rows, :]
            total = total + fy[i, rows, :] + fy[i, above_rows, :] + (z + down(z))
            mask = x_mask
            if j == -1:
                mask = mask * inside[2]
            if j == 4:
                mask = mask * inside[3]
            inverse = (W * mask) / total
            centre[i, rows, :] = total
            scale[i, rows, :] = inverse
            s1[i, rows, :] = inverse * s1[i, rows, :]
        return 0

    lax.fori_loop(1, PLANES - 1, scales, 0)
    smooth(s1, d, fx, fy, fz, scale, spread)

    def image(x, _):
        i = x + HX
        for at, size, j in OWN_CHUNKS:
            here, total = neighbours(d, fx, fy, fz, i, at, size)
            q = centre[i, pl.ds(at, size), :] * here - total
            q_out[x, pl.ds(at - OWN, size), :] = q
            d_out[x, pl.ds(at - OWN, size), :] = here
        return 0

    lax.fori_loop(0, NXL, image, 0)
    for a in range(4):
        for j in range(4):
            rows = pl.ds(32 * j, 32)
            source = q_out[2 * a, rows, :] + q_out[2 * a + 1, rows, :]
            tiles[pl.ds(8 * (4 * a + j), 8), :] = row_group(source)
    tiles[...] = dot(tiles[...], sum_matrix())
    tile = gather_tile(
        [
            [(SOURCE, j, tiles[pl.ds(8 * (4 * a + j), 8), :]) for j in range(4)]
            for a in range(4)
        ]
    )
    tile_out[...] = tile
    for n in range(2):
        xm_lo[pl.ds(128 * n, 128), :] = q_out[n]
        xm_hi[pl.ds(128 * n, 128), :] = q_out[NXL - 2 + n]
    xm_lo[256:264, :] = tile
    xm_hi[256:264, :] = tile


def second_kernel(
    rhs, d0, q0, xlo, xhi, own, below, above, coefs, fx, fy, fz, scale, centre,
    p_out, s_out, dots, s1, d, stack, spread,
):
    zero_pads(s1)
    zero_pads(d)
    mid = stack_tiles(stack, xlo[256:264, :], own[...], xhi[256:264, :])
    low = stack_tiles(stack, below[12], below[13], below[14])
    high = stack_tiles(stack, above[12], above[13], above[14])
    wide = widen(SOURCE, low, mid, high)
    spread_coarse(coarse_sweeps([coefs[k] for k in range(6)], wide), spread)

    def rims(i):
        s1[i, 8:16, :] = scale[i, 8:16, :] * below[i - 1]
        s1[i, 144:152, :] = scale[i, 144:152, :] * above[i - 1]

    def plane(x, _):
        i = x + HX
        s1[i, 16:144, :] = scale[i, 16:144, :] * q0[x]
        rims(i)
        return 0

    lax.fori_loop(0, NXL, plane, 0)
    for n in range(2):
        for i, msg in ((1 + n, xlo), (HX + NXL + n, xhi)):
            s1[i, 16:144, :] = scale[i, 16:144, :] * msg[pl.ds(128 * n, 128), :]
            rims(i)
    smooth(s1, d, fx, fy, fz, scale, spread)

    def image(x, sums):
        i = x + HX
        for at, size, j in OWN_CHUNKS:
            rows = pl.ds(at - OWN, size)
            p, total = neighbours(d, fx, fy, fz, i, at, size)
            s = centre[i, pl.ds(at, size), :] * p - total
            p_out[x, rows, :] = p
            s_out[x, rows, :] = s
            r, dd, q = rhs[x, rows, :], d0[x, rows, :], q0[x, rows, :]
            pairs = ((r, dd), (dd, q), (r, p), (q, p), (dd, s), (p, s))
            sums = tuple(
                acc + row_group(u * v) for acc, (u, v) in zip(sums, pairs)
            )
        return sums

    zero = jnp.zeros((8, NZ), F32)
    sums = lax.fori_loop(0, NXL, image, (zero,) * 6)
    sublane = iota((8, NZ), 0)
    tile = zero
    for n, acc in enumerate(sums):
        tile = jnp.where(sublane == n, jnp.sum(acc, axis=0, keepdims=True), tile)
    for n in range(dots.shape[0]):
        dots[n] = tile


def last_kernel(parts, rhs, d0, q0, p, s, x_out, r_out):
    total = parts[0]
    for n in range(1, parts.shape[0]):
        total = total + parts[n]
    sums = jnp.sum(total, axis=1, keepdims=True)
    rd, dq, rp, qp, ds, ps = [sums[n : n + 1, :] for n in range(6)]
    a0 = rd / dq
    rz = rd - a0 * rp - a0 * dq + a0 * a0 * qp
    ratio = rz / rd
    grow = 1.0 + ratio
    curve = grow * grow * dq - grow * a0 * (ds + qp) + a0 * a0 * ps
    a1 = rz / curve
    u = jnp.broadcast_to(a0 + a1 * grow, (8, NZ))[0:1, :]
    v = jnp.broadcast_to(a1 * a0, (8, NZ))[0:1, :]

    def plane(x, _):
        for at in range(0, NYL, 32):
            rows = pl.ds(at, 32)
            x_out[x, rows, :] = u * d0[x, rows, :] - v * p[x, rows, :]
            r_out[x, rows, :] = rhs[x, rows, :] - u * q0[x, rows, :] + v * s[x, rows, :]
        return 0

    lax.fori_loop(0, NXL, plane, 0)


VMEM = pl.BlockSpec(memory_space=pltpu.VMEM)
SMEM = pl.BlockSpec(memory_space=pltpu.SMEM)


def call(kernel, name, operands, outs, scratch, scalars=0):
    return pl.pallas_call(
        kernel,
        name=name,
        out_shape=[jax.ShapeDtypeStruct(s, F32) for s in outs],
        in_specs=[SMEM] * scalars + [VMEM] * (len(operands) - scalars),
        out_specs=[VMEM] * len(outs),
        scratch_shapes=[pltpu.VMEM(s, F32) for s in scratch],
        compiler_params=pltpu.CompilerParams(vmem_limit_bytes=40 * 1024 * 1024),
    )(*operands)


def upward(values, axis):
    count = lax.axis_size(axis)
    return lax.ppermute(values, axis, [(i, i + 1) for i in range(count - 1)])


def downward(values, axis):
    count = lax.axis_size(axis)
    return lax.ppermute(values, axis, [(i + 1, i) for i in range(count - 1)])


def axis_total(tiles, axis, last=False):
    tiles = lax.all_to_all(tiles, axis, 0, 0)
    if last:
        return tiles
    return tiles.sum(0)


def body(right_side, perm_class, perm_table):
    x_at, y_at = lax.axis_index(X_AXES), lax.axis_index("sy")
    x_end, y_end = lax.axis_size(X_AXES) - 1, lax.axis_size("sy") - 1
    inside = jnp.stack([x_at > 0, x_at < x_end, y_at > 0, y_at < y_end]).astype(F32)
    table = jnp.pad(perm_table, ((0, 6), (0, NZ - perm_table.shape[1])))
    classes = perm_class.astype(F32)
    xlo = upward(jnp.concatenate([classes[-3:], right_side[-2:]]), X_AXES)
    xhi = downward(jnp.concatenate([classes[:3], right_side[:2]]), X_AXES)
    ylo = upward(jnp.concatenate([classes[:, -8:], right_side[:, -8:]]), "sy")
    yhi = downward(jnp.concatenate([classes[:, :8], right_side[:, :8]]), "sy")

    fine = (inside, table, perm_class, right_side, xlo, xhi, ylo, yhi)
    (own,) = call(
        coarse_kernel, "coarse", fine, [(8, NZ)],
        [(NXL + 2, 144, NZ), (56 * 8, NZ), (16 * 8, NZ)], 1,
    )
    left, right = upward(own, X_AXES), downward(own, X_AXES)

    def rim(rows):
        parts = [xlo[:3, rows], xhi[:3, rows], xlo[3:, rows], xhi[3:, rows]]
        return jnp.concatenate(parts + [left[None], own[None], right[None]])

    below = upward(rim(slice(NYL - 8, NYL)), "sy")
    above = downward(rim(slice(0, 8)), "sy")

    block, big = (NXL, NYL, NZ), (PLANES, ROWS, NZ)
    d0, q0, xm_lo, xm_hi, tile, coefs, fx, fy, fz, scale, centre = call(
        first_kernel, "first", fine + (left, own, right, below, above),
        [block, block, (264, NZ), (264, NZ), (8, NZ), (6, 16, NZ)] + [big] * 5,
        [big] * 4 + [(16, NZ), (6, 16, NZ), (16 * 8, NZ)], 1,
    )
    qlo, qhi = upward(xm_hi, X_AXES), downward(xm_lo, X_AXES)

    def rim_q(at):
        parts = [qlo[at : at + 8][None], qlo[128 + at : 136 + at][None], q0[:, at : at + 8]]
        parts += [qhi[at : at + 8][None], qhi[128 + at : 136 + at][None]]
        return jnp.concatenate(parts + [qlo[256:][None], tile[None], qhi[256:][None]])

    below = upward(rim_q(NYL - 8), "sy")
    above = downward(rim_q(0), "sy")
    members = lax.axis_size("cg")
    p, s, dots = call(
        second_kernel, "second",
        (right_side, d0, q0, qlo, qhi, tile, below, above, coefs, fx, fy, fz, scale, centre),
        [block, block, (members, 8, NZ)],
        [big] * 2 + [(16, NZ), (6, 16, NZ)],
    )
    for axis, after in (("cg", "sy"), ("sy", "sx"), ("sx", None)):
        dots = axis_total(dots, axis, after is None)
        if after is not None:
            dots = jnp.broadcast_to(dots[None], (lax.axis_size(after), 8, NZ))
    return tuple(
        call(last_kernel, "last", (dots, right_side, d0, q0, p, s), [block, block], [])
    )


def solution(mesh):
    cells = P(X_AXES, "sy", None)
    return jax.shard_map(
        body,
        mesh=mesh,
        in_specs=(cells, cells, P()),
        out_specs=(cells, cells),
        check_vma=False,
    )
```

```python
import jax
import jax.numpy as jnp
from jax import lax
from jax.experimental import pallas as pl
from jax.experimental.pallas import tpu as pltpu
from jax.sharding import PartitionSpec as P

F32 = jnp.float32
W = 2.0 / 3.0
X_AXES = ("sx", "cg")
SWEEPS = 3

NXL, NYL, NZ = 8, 128, 128
HX = 3
PLANES = NXL + 2 * HX
ROWS = 160
OWN = 16
CHUNKS = ((8, 8, -1), (16, 32, 0), (48, 32, 1), (80, 32, 2), (112, 32, 3), (144, 8, 4))
OWN_CHUNKS = CHUNKS[1:5]
X_LOW, X_HIGH, Y_LOW, Y_HIGH, Z_UP, SOURCE = range(6)


OUTSIDE = 1e-30


def harmonic(a, b):
    return pl.reciprocal(a + b)


def up(v):
    return pltpu.roll(v, NZ - 1, 1)


def down(v):
    return pltpu.roll(v, 1, 1)


def look_up(row, index):
    table = jnp.broadcast_to(row, index.shape)
    return jnp.take_along_axis(table, index, axis=1, mode="promise_in_bounds")


def iota(shape, dim):
    return lax.broadcasted_iota(jnp.int32, shape, dim)


def dot(a, b):
    return jnp.dot(a, b, precision=lax.Precision.HIGHEST, preferred_element_type=F32)


def sum_matrix():
    return jnp.where(iota((NZ, NZ), 0) // 32 == iota((NZ, NZ), 1) % 4, 1.0, 0.0).astype(F32)


def top_matrix():
    lane, col = iota((NZ, NZ), 0), iota((NZ, NZ), 1) % 4
    return jnp.where((lane == 32 * col + 31) & (col < 3), 1.0, 0.0).astype(F32)


def row_group(values):
    return (values[0:8] + values[8:16]) + (values[16:24] + values[24:32])


def gather_tile(pieces):
    group = iota((8, NZ), 1) // 4
    sublane = iota((8, NZ), 0)
    tile = jnp.zeros((8, NZ), F32)
    for a, parts in enumerate(pieces):
        acc = jnp.zeros((8, NZ), F32)
        for field, j, part in parts:
            acc = jnp.where(group == 4 * field + j, part, acc)
        tile = jnp.where(sublane == a, jnp.sum(acc, axis=0, keepdims=True), tile)
    return tile


def own_kernel(table, cls, rhs, kh, kv, fz, tiles):
    khrow, kvrow = 0.5 / table[0:1, :], 0.5 / table[1:2, :]

    def plane(x, _):
        i = x + HX
        for at, size, _j in OWN_CHUNKS:
            rows = pl.ds(at, size)
            index = cls[x, pl.ds(at - OWN, size), :]
            kh[i, rows, :] = look_up(khrow, index)
            k = look_up(kvrow, index)
            kv[i, rows, :] = k
            z = harmonic(k, up(k))
            fz[i, rows, :] = jnp.where(iota((size, NZ), 1) < NZ - 1, z, 0.0)
        return 0

    lax.fori_loop(0, NXL, plane, 0)
    first = iota((8, NZ), 0) == 0
    for f in range(1, 4):
        for j in range(4):
            rows = pl.ds(OWN + 32 * j, 32)
            face = harmonic(kh[2 * f + 2, rows, :], kh[2 * f + 3, rows, :])
            tiles[pl.ds(8 * (4 * (f - 1) + j), 8), :] = row_group(face)
    for a in range(4):
        low, high = 2 * a + HX, 2 * a + HX + 1
        for j in range(1, 4):
            here, under = pl.ds(OWN + 32 * j, 8), pl.ds(OWN + 32 * j - 1, 8)
            total = harmonic(kh[low, under, :], kh[low, here, :])
            total = total + harmonic(kh[high, under, :], kh[high, here, :])
            tiles[pl.ds(8 * (11 + 3 * a + j), 8), :] = jnp.where(first, total, 0.0)
        for j in range(4):
            rows = pl.ds(32 * j, 32)
            source = rhs[2 * a, rows, :] + rhs[2 * a + 1, rows, :]
            tiles[pl.ds(8 * (24 + 4 * a + j), 8), :] = row_group(source)
            rows = pl.ds(OWN + 32 * j, 32)
            upper = fz[low, rows, :] + fz[high, rows, :]
            tiles[pl.ds(8 * (40 + 4 * a + j), 8), :] = row_group(upper)
    tiles[0:320, :] = dot(tiles[0:320, :], sum_matrix())
    tiles[320:448, :] = dot(tiles[320:448, :], top_matrix())


def coarse_kernel(inside, table, xlo, xhi, ylo, yhi, kh, tiles, out, rims):
    khrow = 0.5 / table[0:1, :]

    def rim(classes, side):
        values = look_up(khrow, classes.astype(jnp.int32))
        return jnp.where(inside[side] > 0.5, values, OUTSIDE)

    first = iota((8, NZ), 0) == 0
    for j in range(4):
        rows, own = pl.ds(32 * j, 32), pl.ds(OWN + 32 * j, 32)
        face = harmonic(rim(xlo[2, rows, :], 0), kh[HX, own, :])
        rims[pl.ds(8 * j, 8), :] = row_group(face)
        face = harmonic(kh[HX + NXL - 1, own, :], rim(xhi[0, rows, :], 1))
        rims[pl.ds(8 * (4 + j), 8), :] = row_group(face)
    for a in range(4):
        low = high = jnp.zeros((8, NZ), F32)
        for x in (2 * a, 2 * a + 1):
            i = x + HX
            under = pltpu.roll(rim(ylo[x], 2), 1, 0)
            low = low + harmonic(under, kh[i, OWN : OWN + 8, :])
            high = high + harmonic(kh[i, 143:151, :], rim(yhi[x], 3))
        rims[pl.ds(8 * (8 + a), 8), :] = jnp.where(first, low, 0.0)
        rims[pl.ds(8 * (12 + a), 8), :] = jnp.where(first, high, 0.0)
    rims[...] = dot(rims[...], sum_matrix())

    def inner(t):
        return tiles[pl.ds(8 * t, 8), :]

    def outer(t):
        return rims[pl.ds(8 * t, 8), :]

    def x_face(f, j):
        return outer(f + j) if f in (0, 4) else inner(4 * (f - 1) + j)

    def y_face(a, j):
        return outer(8 + a + j) if j in (0, 4) else inner(11 + 3 * a + j)

    pieces = []
    for a in range(4):
        parts = []
        for j in range(4):
            parts += [
                (X_LOW, j, x_face(a, j)),
                (X_HIGH, j, x_face(a + 1, j)),
                (Y_LOW, j, y_face(a, j)),
                (Y_HIGH, j, y_face(a, j + 1)),
                (Z_UP, j, inner(40 + 4 * a + j)),
                (SOURCE, j, inner(24 + 4 * a + j)),
            ]
        pieces.append(parts)
    out[...] = gather_tile(pieces)


def stack_tiles(buf, left, own, right):
    buf[0:4, :] = left[0:4, :]
    buf[4:8, :] = own[0:4, :]
    buf[8:12, :] = right[0:4, :]
    buf[12:16, :] = jnp.zeros((4, NZ), F32)
    return buf[...]


def widen(field, below, own, above):
    lane = iota((16, NZ), 1)

    def placed(v, at):
        shift = (at - 16 * field) % NZ
        return pltpu.roll(v, shift, 1) if shift else v

    wide = jnp.where(lane < 16, placed(below, 0), placed(own, 16))
    wide = jnp.where(lane < 32, wide, placed(above, 32))
    return jnp.where(lane < 48, wide, 0.0)


def coarse_sweeps(coefs, source):
    x_low, x_high, y_low, y_high, z_up, scale = coefs
    start = scale * source
    c = start
    for _ in range(SWEEPS):
        beside = x_low * pltpu.roll(c, 1, 0) + x_high * pltpu.roll(c, 15, 0)
        beside = beside + y_low * pltpu.roll(c, 4, 1) + y_high * pltpu.roll(c, NZ - 4, 1)
        beside = beside + z_up * up(c) + down(z_up * c)
        c = (1.0 - W) * c + (start + scale * beside)
    return c


def spread_coarse(c, spread):
    for k in range(6):
        lane = iota((NZ, NZ), 1)
        pick = jnp.where(iota((NZ, NZ), 0) == 4 * (k + 3) + lane // 32, 1.0, 0.0)
        spread[k] = dot(c, pick.astype(F32))


def neighbours(v, fx, fy, fz, i, at, size):
    here = v[i, pl.ds(at, size), :]
    total = fx[i, pl.ds(at, size), :] * v[i - 1, pl.ds(at, size), :]
    total = total + fx[i + 1, pl.ds(at, size), :] * v[i + 1, pl.ds(at, size), :]
    total = total + fy[i, pl.ds(at, size), :] * v[i, pl.ds(at - 1, size), :]
    total = total + fy[i, pl.ds(at + 1, size), :] * v[i, pl.ds(at + 1, size), :]
    z = fz[i, pl.ds(at, size), :]
    return here, total + z * up(here) + down(z * here)


def smooth_chunk(s1, d, fx, fy, fz, scale, spread, i, at, size, j):
    here, total = neighbours(s1, fx, fy, fz, i, at, size)
    value = (2.0 - W) * here + scale[i, pl.ds(at, size), :] * total
    if spread is not None:
        value = value + spread[j + 1, pl.ds((i + 5) // 2, 1), :]
    d[i, pl.ds(at, size), :] = value


def zero_pads(v):
    def plane(i, _):
        v[i, 0:8, :] = jnp.zeros((8, NZ), F32)
        v[i, ROWS - 8 : ROWS, :] = jnp.zeros((8, NZ), F32)
        return 0

    lax.fori_loop(0, PLANES, plane, 0)


def looked_up(inside, table, kh, kv, i, at, size, classes, *sides):
    index = classes.astype(jnp.int32)
    values = look_up(0.5 / table[0:1, :], index)
    for side in sides:
        values = jnp.where(inside[side] > 0.5, values, OUTSIDE)
    kh[i, pl.ds(at, size), :] = values
    if 0 < i < PLANES - 1 if isinstance(i, int) else True:
        kv[i, pl.ds(at, size), :] = look_up(0.5 / table[1:2, :], index)


def set_scale(i, at, size, mask, source, fx, fy, fz, scale, centre, s1):
    rows = pl.ds(at, size)
    z = fz[i, rows, :]
    total = fx[i, rows, :] + fx[i + 1, rows, :]
    total = total + fy[i, rows, :] + fy[i, pl.ds(at + 1, size), :] + (z + down(z))
    inverse = (W * mask) * pl.reciprocal(total)
    scale[i, rows, :] = inverse
    s1[i, rows, :] = inverse * source
    if centre is not None:
        centre[i, rows, :] = total


def cells_kernel(
    inside, table, rhs, xlo, xhi, ylo, yhi, _kh, _kv, fz,
    kh, kv, fx, fy, scale, centre, s1,
):
    def rims(x, _):
        looked_up(inside, table, kh, kv, x + HX, 8, 8, ylo[x], 2)
        looked_up(inside, table, kh, kv, x + HX, 144, 8, yhi[x], 3)
        return 0

    lax.fori_loop(0, NXL, rims, 0)
    for n in range(3):
        for side, base, msg in ((0, 0, xlo), (1, HX + NXL, xhi)):
            looked_up(inside, table, kh, kv, base + n, OWN, NYL, msg[n], side)

    def faces(i, _):
        for at, size, j in OWN_CHUNKS:
            rows = pl.ds(at, size)
            here = kh[i, rows, :]
            fx[i, rows, :] = harmonic(kh[i - 1, rows, :], here)
            fy[i, rows, :] = harmonic(kh[i, pl.ds(at - 1, size), :], here)
        fy[i, 144:152, :] = harmonic(kh[i, 143:151, :], kh[i, 144:152, :])
        return 0

    lax.fori_loop(HX, HX + NXL, faces, 0)
    end = HX + NXL
    fx[end, 16:144, :] = harmonic(kh[end - 1, 16:144, :], kh[end, 16:144, :])

    def scales(x, _):
        for at, size, j in OWN_CHUNKS:
            source = rhs[x, pl.ds(at - OWN, size), :]
            set_scale(x + HX, at, size, 1.0, source, fx, fy, fz, scale, centre, s1)
        return 0

    lax.fori_loop(0, NXL, scales, 0)


RIM_PLANES = (1, 2, HX + NXL, HX + NXL + 1)
RIM_CHUNKS = (CHUNKS[0], CHUNKS[5])


def first_kernel(
    inside, table, xlo, xhi, ylo, yhi, left, own, right, below, above, centre,
    _kh, _kv, _fx, _fy, _fz, _scale, _s1,
    d_out, q_out, xm_lo, xm_hi, tile_out, coefs_out, kh, kv, fx, fy, fz, scale, s1,
    d, stack, spread, tiles,
):
    for n in range(3):
        for side, i in ((0, n), (1, HX + NXL + n)):
            corner = 3 * side + n
            looked_up(inside, table, kh, kv, i, 8, 8, below[corner], side, 2)
            looked_up(inside, table, kh, kv, i, 144, 8, above[corner], side, 3)

    def pads(i, _):
        ones = jnp.ones((8, NZ), F32)
        kh[i, 0:8, :] = ones
        kh[i, ROWS - 8 : ROWS, :] = ones
        fy[i, ROWS - 8 : ROWS, :] = ones
        return 0

    lax.fori_loop(0, PLANES, pads, 0)
    zero_pads(s1)
    zero_pads(d)

    mid = stack_tiles(stack, left, own, right)
    low = stack_tiles(stack, below[10], below[11], below[12])
    high = stack_tiles(stack, above[10], above[11], above[12])
    wide = [widen(k, low, mid, high) for k in range(6)]
    total = wide[0] + wide[1] + wide[2] + wide[3] + wide[4] + down(wide[4])
    valid = total > 0.0
    wide_scale = jnp.where(valid, W / jnp.where(valid, total, 1.0), 0.0)
    coefs = wide[:5] + [wide_scale]
    for k in range(6):
        coefs_out[k] = coefs[k]
    spread_coarse(coarse_sweeps(coefs, wide[SOURCE]), spread)

    def set_faces(i, at, size):
        rows = pl.ds(at, size)
        here = kh[i, rows, :]
        fx[i, rows, :] = harmonic(kh[i - 1, rows, :], here)
        fy[i, rows, :] = harmonic(kh[i, pl.ds(at - 1, size), :], here)
        k = kv[i, rows, :]
        z = harmonic(k, up(k))
        fz[i, rows, :] = jnp.where(iota((size, NZ), 1) < NZ - 1, z, 0.0)

    def rim_faces(i, _):
        for at, size, _j in RIM_CHUNKS:
            set_faces(i, at, size)
        return 0

    lax.fori_loop(1, PLANES - 1, rim_faces, 0)
    for i in RIM_PLANES:
        for at, size, _j in OWN_CHUNKS:
            set_faces(i, at, size)
    last = PLANES - 1
    for at, size, _j in CHUNKS:
        rows = pl.ds(at, size)
        fx[last, rows, :] = harmonic(kh[last - 1, rows, :], kh[last, rows, :])

    def rim_scales(i, mask, source_low, source_high):
        set_scale(i, 8, 8, mask * inside[2], source_low, fx, fy, fz, scale, None, s1)
        set_scale(i, 144, 8, mask * inside[3], source_high, fx, fy, fz, scale, None, s1)

    def own_rims(x, _):
        rim_scales(x + HX, 1.0, ylo[NXL + x], yhi[NXL + x])
        return 0

    lax.fori_loop(0, NXL, own_rims, 0)
    for n in range(2):
        for side, i, msg in ((0, 1 + n, xlo), (1, HX + NXL + n, xhi)):
            corner = 6 + 2 * side + n
            rim_scales(i, inside[side], below[corner], above[corner])
            for at, size, _j in OWN_CHUNKS:
                source = msg[3 + n, pl.ds(at - OWN, size), :]
                set_scale(i, at, size, inside[side], source, fx, fy, fz, scale, None, s1)

    def smooth(i, _):
        for at, size, j in CHUNKS:
            smooth_chunk(s1, d, fx, fy, fz, scale, spread, i, at, size, j)
        return 0

    lax.fori_loop(HX - 1, HX + NXL + 1, smooth, 0)

    def image(x, _):
        i = x + HX
        for at, size, j in OWN_CHUNKS:
            here, total = neighbours(d, fx, fy, fz, i, at, size)
            q = centre[i, pl.ds(at, size), :] * here - total
            q_out[x, pl.ds(at - OWN, size), :] = q
            d_out[x, pl.ds(at - OWN, size), :] = here
        return 0

    lax.fori_loop(0, NXL, image, 0)
    for a in range(4):
        for j in range(4):
            rows = pl.ds(32 * j, 32)
            source = q_out[2 * a, rows, :] + q_out[2 * a + 1, rows, :]
            tiles[pl.ds(8 * (4 * a + j), 8), :] = row_group(source)
    tiles[...] = dot(tiles[...], sum_matrix())
    tile = gather_tile(
        [
            [(SOURCE, j, tiles[pl.ds(8 * (4 * a + j), 8), :]) for j in range(4)]
            for a in range(4)
        ]
    )
    tile_out[...] = tile
    for n in range(2):
        xm_lo[pl.ds(128 * n, 128), :] = q_out[n]
        xm_hi[pl.ds(128 * n, 128), :] = q_out[NXL - 2 + n]
    xm_lo[256:264, :] = tile
    xm_hi[256:264, :] = tile


INNER_CHUNKS = ((24, 24, 0), (48, 32, 1), (80, 32, 2), (112, 24, 3))
OUTER_CHUNKS = ((8, 8, -1), (16, 8, 0), (136, 8, 3), (144, 8, 4))


def inner_kernel(rhs, d0, q0, fx, fy, fz, scale, s1, d, known):
    zero_pads(s1)
    zero_pads(d)

    def plane(x, sums):
        i = x + HX
        for at, size, j in OWN_CHUNKS:
            rows = pl.ds(at - OWN, size)
            q = q0[x, rows, :]
            s1[i, pl.ds(at, size), :] = scale[i, pl.ds(at, size), :] * q
            dd = d0[x, rows, :]
            rd, dq = sums
            sums = (rd + row_group(rhs[x, rows, :] * dd), dq + row_group(dd * q))
        return sums

    zero = jnp.zeros((8, NZ), F32)
    rd, dq = lax.fori_loop(0, NXL, plane, (zero, zero))
    known[0:8, :] = rd
    known[8:16, :] = dq

    def smooth(i, _):
        for at, size, j in INNER_CHUNKS:
            smooth_chunk(s1, d, fx, fy, fz, scale, None, i, at, size, j)
        return 0

    lax.fori_loop(HX + 1, HX + NXL - 1, smooth, 0)


def second_kernel(
    rhs, d0, q0, xlo, xhi, own, below, above, coefs, fx, fy, fz, scale, centre, known,
    _s1, _d, p_out, s_out, dots, s1, d, stack, spread,
):
    mid = stack_tiles(stack, xlo[256:264, :], own[...], xhi[256:264, :])
    low = stack_tiles(stack, below[12], below[13], below[14])
    high = stack_tiles(stack, above[12], above[13], above[14])
    wide = widen(SOURCE, low, mid, high)
    spread_coarse(coarse_sweeps([coefs[k] for k in range(6)], wide), spread)

    def rims(i, _):
        s1[i, 8:16, :] = scale[i, 8:16, :] * below[i - 1]
        s1[i, 144:152, :] = scale[i, 144:152, :] * above[i - 1]
        return 0

    lax.fori_loop(1, PLANES - 1, rims, 0)
    for n in range(2):
        for i, msg in ((1 + n, xlo), (HX + NXL + n, xhi)):
            s1[i, 16:144, :] = scale[i, 16:144, :] * msg[pl.ds(128 * n, 128), :]

    for i in (HX - 1, HX, HX + NXL - 1, HX + NXL):
        for at, size, j in CHUNKS:
            smooth_chunk(s1, d, fx, fy, fz, scale, spread, i, at, size, j)

    def smooth(i, _):
        for at, size, j in OUTER_CHUNKS:
            smooth_chunk(s1, d, fx, fy, fz, scale, spread, i, at, size, j)
        for at, size, j in INNER_CHUNKS:
            rows = pl.ds(at, size)
            d[i, rows, :] = d[i, rows, :] + spread[j + 1, pl.ds((i + 5) // 2, 1), :]
        return 0

    lax.fori_loop(HX + 1, HX + NXL - 1, smooth, 0)

    def image(x, sums):
        i = x + HX
        for at, size, j in OWN_CHUNKS:
            rows = pl.ds(at - OWN, size)
            p, total = neighbours(d, fx, fy, fz, i, at, size)
            s = centre[i, pl.ds(at, size), :] * p - total
            p_out[x, rows, :] = p
            s_out[x, rows, :] = s
            r, dd, q = rhs[x, rows, :], d0[x, rows, :], q0[x, rows, :]
            pairs = ((r, p), (q, p), (dd, s), (p, s))
            sums = tuple(
                acc + row_group(u * v) for acc, (u, v) in zip(sums, pairs)
            )
        return sums

    zero = jnp.zeros((8, NZ), F32)
    sums = lax.fori_loop(0, NXL, image, (zero,) * 4)
    sums = (known[0:8, :], known[8:16, :]) + sums
    sublane, lane = iota((8, NZ), 0), iota((8, NZ), 1)
    tile = zero
    for n, acc in enumerate(sums):
        tile = jnp.where(sublane == n, jnp.sum(acc, axis=0, keepdims=True), tile)
    tile = jnp.where(sublane == lane, jnp.sum(tile, axis=1, keepdims=True), 0.0)
    dots[...] = jnp.sum(tile, axis=0, keepdims=True)


def last_kernel(parts, rhs, d0, q0, p, s, x_out, r_out):
    total = parts[0:8, :]
    for n in range(8, parts.shape[0], 8):
        total = total + parts[n : n + 8, :]
    sums = jnp.sum(total, axis=0, keepdims=True)
    rd, dq, rp, qp, ds, ps = [sums[:, n : n + 1] for n in range(6)]
    a0 = rd / dq
    rz = rd - a0 * rp - a0 * dq + a0 * a0 * qp
    ratio = rz / rd
    grow = 1.0 + ratio
    curve = grow * grow * dq - grow * a0 * (ds + qp) + a0 * a0 * ps
    a1 = rz / curve
    u = jnp.broadcast_to(a0 + a1 * grow, (8, NZ))[0:1, :]
    v = jnp.broadcast_to(a1 * a0, (8, NZ))[0:1, :]

    def plane(x, _):
        for at in range(0, NYL, 32):
            rows = pl.ds(at, 32)
            x_out[x, rows, :] = u * d0[x, rows, :] - v * p[x, rows, :]
            r_out[x, rows, :] = rhs[x, rows, :] - u * q0[x, rows, :] + v * s[x, rows, :]
        return 0

    lax.fori_loop(0, NXL, plane, 0)


VMEM = pl.BlockSpec(memory_space=pltpu.VMEM)
SMEM = pl.BlockSpec(memory_space=pltpu.SMEM)


def call(kernel, name, operands, outs, scratch, scalars=0, aliases=None):
    return pl.pallas_call(
        kernel,
        name=name,
        out_shape=[jax.ShapeDtypeStruct(s, F32) for s in outs],
        in_specs=[SMEM] * scalars + [VMEM] * (len(operands) - scalars),
        out_specs=[VMEM] * len(outs),
        scratch_shapes=[pltpu.VMEM(s, F32) for s in scratch],
        input_output_aliases=aliases or {},
        compiler_params=pltpu.CompilerParams(vmem_limit_bytes=24 * 1024 * 1024),
    )(*operands)


def upward(values, axis):
    count = lax.axis_size(axis)
    return lax.ppermute(values, axis, [(i, i + 1) for i in range(count - 1)])


def downward(values, axis):
    count = lax.axis_size(axis)
    return lax.ppermute(values, axis, [(i + 1, i) for i in range(count - 1)])


def exchange(row, axes):
    count = lax.axis_size(axes)
    rows = jnp.broadcast_to(row[None], (count, 1, NZ))
    return lax.all_to_all(rows, axes, 0, 0).reshape(count, NZ)


STAGES = (("sy", "cg"), "sx")


def body(right_side, perm_class, perm_table):
    x_at, y_at = lax.axis_index(X_AXES), lax.axis_index("sy")
    x_end, y_end = lax.axis_size(X_AXES) - 1, lax.axis_size("sy") - 1
    inside = jnp.stack([x_at > 0, x_at < x_end, y_at > 0, y_at < y_end]).astype(F32)
    pad = ((0, 6), (0, NZ - perm_table.shape[1]))
    table = jnp.pad(perm_table, pad, constant_values=1.0)

    def packed(classes, values):
        return jnp.concatenate([classes.astype(F32), values])

    xlo = upward(packed(perm_class[-3:], right_side[-2:]), X_AXES)
    xhi = downward(packed(perm_class[:3], right_side[:2]), X_AXES)
    ylo = upward(packed(perm_class[:, -8:], right_side[:, -8:]), "sy")
    yhi = downward(packed(perm_class[:, :8], right_side[:, :8]), "sy")

    block, big = (NXL, NYL, NZ), (PLANES, ROWS, NZ)
    kh, kv, fz, tiles = call(
        own_kernel, "own", (table, perm_class, right_side), [big] * 3 + [(448, NZ)], []
    )
    halos = (xlo, xhi, ylo, yhi)
    (own,) = call(
        coarse_kernel, "coarse", (inside, table) + halos + (kh, tiles), [(8, NZ)],
        [(128, NZ)], 1,
    )
    kh, kv, fx, fy, scale, centre, s1 = call(
        cells_kernel, "cells", (inside, table, right_side) + halos + (kh, kv, fz),
        [big] * 7, [], 1, {7: 0, 8: 1},
    )
    left, right = upward(own, X_AXES), downward(own, X_AXES)

    def rim(rows):
        parts = [xlo[:3, rows], xhi[:3, rows], xlo[3:, rows], xhi[3:, rows]]
        return jnp.concatenate(parts + [left[None], own[None], right[None]])

    below = upward(rim(slice(NYL - 8, NYL)), "sy")
    above = downward(rim(slice(0, 8)), "sy")

    d0, q0, xm_lo, xm_hi, tile, coefs, _, _, fx, fy, fz, scale, _ = call(
        first_kernel, "first",
        (inside, table) + halos + (left, own, right, below, above, centre)
        + (kh, kv, fx, fy, fz, scale, s1),
        [block, block, (264, NZ), (264, NZ), (8, NZ), (6, 16, NZ)] + [big] * 7,
        [big, (16, NZ), (6, 16, NZ), (16 * 8, NZ)], 1,
        {12 + n: 6 + n for n in range(7)},
    )
    qlo, qhi = upward(xm_hi, X_AXES), downward(xm_lo, X_AXES)
    s1, d, known = call(
        inner_kernel, "inner", (right_side, d0, q0, fx, fy, fz, scale),
        [big, big, (16, NZ)], [],
    )

    def rim_q(at):
        parts = [qlo[at : at + 8][None], qlo[128 + at : 136 + at][None], q0[:, at : at + 8]]
        parts += [qhi[at : at + 8][None], qhi[128 + at : 136 + at][None]]
        return jnp.concatenate(parts + [qlo[256:][None], tile[None], qhi[256:][None]])

    below = upward(rim_q(NYL - 8), "sy")
    above = downward(rim_q(0), "sy")
    p, s, dots, _, _ = call(
        second_kernel, "second",
        (right_side, d0, q0, qlo, qhi, tile, below, above, coefs, fx, fy, fz, scale, centre)
        + (known, s1, d),
        [block, block, (1, NZ), big, big], [(16, NZ), (6, 16, NZ)], 0, {15: 3, 16: 4},
    )
    for axes in STAGES[:-1]:
        dots = exchange(dots, axes).sum(0, keepdims=True)
    dots = exchange(dots, STAGES[-1])
    return tuple(
        call(last_kernel, "last", (dots, right_side, d0, q0, p, s), [block, block], [])
    )


def solution(mesh):
    cells = P(X_AXES, "sy", None)
    return jax.shard_map(
        body,
        mesh=mesh,
        in_specs=(cells, cells, P()),
        out_specs=(cells, cells),
        check_vma=False,
    )
```

```python
import jax
import jax.numpy as jnp
from jax import lax
from jax.experimental import pallas as pl
from jax.experimental.pallas import tpu as pltpu
from jax.sharding import PartitionSpec as P

F32 = jnp.float32
W = 2.0 / 3.0
X_AXES = ("sx", "cg")
SWEEPS = 3

NXL, NYL, NZ = 8, 128, 128
HX = 3
PLANES = NXL + 2 * HX
ROWS = 160
OWN = 16
CHUNKS = ((8, 8, -1), (16, 32, 0), (48, 32, 1), (80, 32, 2), (112, 32, 3), (144, 8, 4))
OWN_CHUNKS = CHUNKS[1:5]
X_LOW, X_HIGH, Y_LOW, Y_HIGH, Z_UP, SOURCE = range(6)


OUTSIDE = 1e-30


def harmonic(a, b):
    return pl.reciprocal(a + b)


def up(v):
    return pltpu.roll(v, NZ - 1, 1)


def down(v):
    return pltpu.roll(v, 1, 1)


def look_up(row, index):
    table = jnp.broadcast_to(row, index.shape)
    return jnp.take_along_axis(table, index, axis=1, mode="promise_in_bounds")


def iota(shape, dim):
    return lax.broadcasted_iota(jnp.int32, shape, dim)


def dot(a, b):
    return jnp.dot(a, b, precision=lax.Precision.HIGHEST, preferred_element_type=F32)


def sum_matrix():
    return jnp.where(iota((NZ, NZ), 0) // 32 == iota((NZ, NZ), 1) % 4, 1.0, 0.0).astype(F32)


def top_matrix():
    lane, col = iota((NZ, NZ), 0), iota((NZ, NZ), 1) % 4
    return jnp.where((lane == 32 * col + 31) & (col < 3), 1.0, 0.0).astype(F32)


def row_group(values):
    return (values[0:8] + values[8:16]) + (values[16:24] + values[24:32])


def gather_tile(pieces):
    group = iota((8, NZ), 1) // 4
    sublane = iota((8, NZ), 0)
    tile = jnp.zeros((8, NZ), F32)
    for a, parts in enumerate(pieces):
        acc = jnp.zeros((8, NZ), F32)
        for field, j, part in parts:
            acc = jnp.where(group == 4 * field + j, part, acc)
        tile = jnp.where(sublane == a, jnp.sum(acc, axis=0, keepdims=True), tile)
    return tile


def own_kernel(table, cls, rhs, kh, kv, fz, tiles):
    khrow, kvrow = 0.5 / table[0:1, :], 0.5 / table[1:2, :]

    def plane(x, _):
        i = x + HX
        for at, size, _j in OWN_CHUNKS:
            rows = pl.ds(at, size)
            index = cls[x, pl.ds(at - OWN, size), :]
            kh[i, rows, :] = look_up(khrow, index)
            k = look_up(kvrow, index)
            kv[i, rows, :] = k
            z = harmonic(k, up(k))
            fz[i, rows, :] = jnp.where(iota((size, NZ), 1) < NZ - 1, z, 0.0)
        return 0

    lax.fori_loop(0, NXL, plane, 0)
    first = iota((8, NZ), 0) == 0
    for f in range(1, 4):
        for j in range(4):
            rows = pl.ds(OWN + 32 * j, 32)
            face = harmonic(kh[2 * f + 2, rows, :], kh[2 * f + 3, rows, :])
            tiles[pl.ds(8 * (4 * (f - 1) + j), 8), :] = row_group(face)
    for a in range(4):
        low, high = 2 * a + HX, 2 * a + HX + 1
        for j in range(1, 4):
            here, under = pl.ds(OWN + 32 * j, 8), pl.ds(OWN + 32 * j - 1, 8)
            total = harmonic(kh[low, under, :], kh[low, here, :])
            total = total + harmonic(kh[high, under, :], kh[high, here, :])
            tiles[pl.ds(8 * (11 + 3 * a + j), 8), :] = jnp.where(first, total, 0.0)
        for j in range(4):
            rows = pl.ds(32 * j, 32)
            source = rhs[2 * a, rows, :] + rhs[2 * a + 1, rows, :]
            tiles[pl.ds(8 * (24 + 4 * a + j), 8), :] = row_group(source)
            rows = pl.ds(OWN + 32 * j, 32)
            upper = fz[low, rows, :] + fz[high, rows, :]
            tiles[pl.ds(8 * (40 + 4 * a + j), 8), :] = row_group(upper)
    tiles[0:320, :] = dot(tiles[0:320, :], sum_matrix())
    tiles[320:448, :] = dot(tiles[320:448, :], top_matrix())


def coarse_kernel(inside, table, xlo, xhi, ylo, yhi, kh, tiles, out, rims):
    khrow = 0.5 / table[0:1, :]

    def rim(classes, side):
        values = look_up(khrow, classes.astype(jnp.int32))
        return jnp.where(inside[side] > 0.5, values, OUTSIDE)

    first = iota((8, NZ), 0) == 0
    for j in range(4):
        rows, own = pl.ds(32 * j, 32), pl.ds(OWN + 32 * j, 32)
        face = harmonic(rim(xlo[2, rows, :], 0), kh[HX, own, :])
        rims[pl.ds(8 * j, 8), :] = row_group(face)
        face = harmonic(kh[HX + NXL - 1, own, :], rim(xhi[0, rows, :], 1))
        rims[pl.ds(8 * (4 + j), 8), :] = row_group(face)
    for a in range(4):
        low = high = jnp.zeros((8, NZ), F32)
        for x in (2 * a, 2 * a + 1):
            i = x + HX
            under = pltpu.roll(rim(ylo[x], 2), 1, 0)
            low = low + harmonic(under, kh[i, OWN : OWN + 8, :])
            high = high + harmonic(kh[i, 143:151, :], rim(yhi[x], 3))
        rims[pl.ds(8 * (8 + a), 8), :] = jnp.where(first, low, 0.0)
        rims[pl.ds(8 * (12 + a), 8), :] = jnp.where(first, high, 0.0)
    rims[...] = dot(rims[...], sum_matrix())

    def inner(t):
        return tiles[pl.ds(8 * t, 8), :]

    def outer(t):
        return rims[pl.ds(8 * t, 8), :]

    def x_face(f, j):
        return outer(f + j) if f in (0, 4) else inner(4 * (f - 1) + j)

    def y_face(a, j):
        return outer(8 + a + j) if j in (0, 4) else inner(11 + 3 * a + j)

    pieces = []
    for a in range(4):
        parts = []
        for j in range(4):
            parts += [
                (X_LOW, j, x_face(a, j)),
                (X_HIGH, j, x_face(a + 1, j)),
                (Y_LOW, j, y_face(a, j)),
                (Y_HIGH, j, y_face(a, j + 1)),
                (Z_UP, j, inner(40 + 4 * a + j)),
                (SOURCE, j, inner(24 + 4 * a + j)),
            ]
        pieces.append(parts)
    out[...] = gather_tile(pieces)


def stack_tiles(buf, left, own, right):
    buf[0:4, :] = left[0:4, :]
    buf[4:8, :] = own[0:4, :]
    buf[8:12, :] = right[0:4, :]
    buf[12:16, :] = jnp.zeros((4, NZ), F32)
    return buf[...]


def widen(field, below, own, above):
    lane = iota((16, NZ), 1)

    def placed(v, at):
        shift = (at - 16 * field) % NZ
        return pltpu.roll(v, shift, 1) if shift else v

    wide = jnp.where(lane < 16, placed(below, 0), placed(own, 16))
    wide = jnp.where(lane < 32, wide, placed(above, 32))
    return jnp.where(lane < 48, wide, 0.0)


def coarse_sweeps(coefs, source):
    x_low, x_high, y_low, y_high, z_up, scale = coefs
    start = scale * source
    c = start
    for _ in range(SWEEPS):
        beside = x_low * pltpu.roll(c, 1, 0) + x_high * pltpu.roll(c, 15, 0)
        beside = beside + y_low * pltpu.roll(c, 4, 1) + y_high * pltpu.roll(c, NZ - 4, 1)
        beside = beside + z_up * up(c) + down(z_up * c)
        c = (1.0 - W) * c + (start + scale * beside)
    return c


def spread_coarse(c, spread):
    for k in range(6):
        lane = iota((NZ, NZ), 1)
        pick = jnp.where(iota((NZ, NZ), 0) == 4 * (k + 3) + lane // 32, 1.0, 0.0)
        spread[k] = dot(c, pick.astype(F32))


def neighbours(v, fx, fy, fz, i, at, size):
    here = v[i, pl.ds(at, size), :]
    total = fx[i, pl.ds(at, size), :] * v[i - 1, pl.ds(at, size), :]
    total = total + fx[i + 1, pl.ds(at, size), :] * v[i + 1, pl.ds(at, size), :]
    total = total + fy[i, pl.ds(at, size), :] * v[i, pl.ds(at - 1, size), :]
    total = total + fy[i, pl.ds(at + 1, size), :] * v[i, pl.ds(at + 1, size), :]
    z = fz[i, pl.ds(at, size), :]
    return here, total + z * up(here) + down(z * here)


def smooth_chunk(s1, d, fx, fy, fz, scale, spread, i, at, size, j):
    here, total = neighbours(s1, fx, fy, fz, i, at, size)
    value = (2.0 - W) * here + scale[i, pl.ds(at, size), :] * total
    if spread is not None:
        value = value + spread[j + 1, pl.ds((i + 5) // 2, 1), :]
    d[i, pl.ds(at, size), :] = value


def zero_pads(v):
    def plane(i, _):
        v[i, 0:8, :] = jnp.zeros((8, NZ), F32)
        v[i, ROWS - 8 : ROWS, :] = jnp.zeros((8, NZ), F32)
        return 0

    lax.fori_loop(0, PLANES, plane, 0)


def looked_up(inside, table, kh, kv, i, at, size, classes, *sides):
    index = classes.astype(jnp.int32)
    values = look_up(0.5 / table[0:1, :], index)
    for side in sides:
        values = jnp.where(inside[side] > 0.5, values, OUTSIDE)
    kh[i, pl.ds(at, size), :] = values
    if 0 < i < PLANES - 1 if isinstance(i, int) else True:
        kv[i, pl.ds(at, size), :] = look_up(0.5 / table[1:2, :], index)


def set_scale(i, at, size, mask, source, fx, fy, fz, scale, centre, s1):
    rows = pl.ds(at, size)
    z = fz[i, rows, :]
    total = fx[i, rows, :] + fx[i + 1, rows, :]
    total = total + fy[i, rows, :] + fy[i, pl.ds(at + 1, size), :] + (z + down(z))
    inverse = (W * mask) * pl.reciprocal(total)
    scale[i, rows, :] = inverse
    s1[i, rows, :] = inverse * source
    if centre is not None:
        centre[i, rows, :] = total


def cells_kernel(
    inside, table, rhs, xlo, xhi, ylo, yhi, _kh, _kv, fz,
    kh, kv, fx, fy, scale, centre, s1,
):
    def rims(x, _):
        looked_up(inside, table, kh, kv, x + HX, 8, 8, ylo[x], 2)
        looked_up(inside, table, kh, kv, x + HX, 144, 8, yhi[x], 3)
        return 0

    lax.fori_loop(0, NXL, rims, 0)
    for n in range(3):
        for side, base, msg in ((0, 0, xlo), (1, HX + NXL, xhi)):
            looked_up(inside, table, kh, kv, base + n, OWN, NYL, msg[n], side)

    def faces(i, _):
        for at, size, j in OWN_CHUNKS:
            rows = pl.ds(at, size)
            here = kh[i, rows, :]
            fx[i, rows, :] = harmonic(kh[i - 1, rows, :], here)
            fy[i, rows, :] = harmonic(kh[i, pl.ds(at - 1, size), :], here)
        fy[i, 144:152, :] = harmonic(kh[i, 143:151, :], kh[i, 144:152, :])
        return 0

    lax.fori_loop(HX, HX + NXL, faces, 0)
    end = HX + NXL
    fx[end, 16:144, :] = harmonic(kh[end - 1, 16:144, :], kh[end, 16:144, :])

    def scales(x, _):
        for at, size, j in OWN_CHUNKS:
            source = rhs[x, pl.ds(at - OWN, size), :]
            set_scale(x + HX, at, size, 1.0, source, fx, fy, fz, scale, centre, s1)
        return 0

    lax.fori_loop(0, NXL, scales, 0)


RIM_PLANES = (1, 2, HX + NXL, HX + NXL + 1)
RIM_CHUNKS = (CHUNKS[0], CHUNKS[5])


def first_kernel(
    inside, table, xlo, xhi, ylo, yhi, left, own, right, below, above, centre,
    _kh, _kv, _fx, _fy, _fz, _scale, _s1,
    d_out, q_out, q_far, q_near, tile_out, coefs_out, kh, kv, fx, fy, fz, scale, s1,
    d, stack, spread, tiles,
):
    for n in range(3):
        for side, i in ((0, n), (1, HX + NXL + n)):
            corner = 3 * side + n
            looked_up(inside, table, kh, kv, i, 8, 8, below[corner], side, 2)
            looked_up(inside, table, kh, kv, i, 144, 8, above[corner], side, 3)

    def pads(i, _):
        ones = jnp.ones((8, NZ), F32)
        kh[i, 0:8, :] = ones
        kh[i, ROWS - 8 : ROWS, :] = ones
        fy[i, ROWS - 8 : ROWS, :] = ones
        return 0

    lax.fori_loop(0, PLANES, pads, 0)
    zero_pads(s1)
    zero_pads(d)

    mid = stack_tiles(stack, left, own, right)
    low = stack_tiles(stack, below[10], below[11], below[12])
    high = stack_tiles(stack, above[10], above[11], above[12])
    wide = [widen(k, low, mid, high) for k in range(6)]
    total = wide[0] + wide[1] + wide[2] + wide[3] + wide[4] + down(wide[4])
    valid = total > 0.0
    wide_scale = jnp.where(valid, W / jnp.where(valid, total, 1.0), 0.0)
    coefs = wide[:5] + [wide_scale]
    for k in range(6):
        coefs_out[k] = coefs[k]
    spread_coarse(coarse_sweeps(coefs, wide[SOURCE]), spread)

    def set_faces(i, at, size):
        rows = pl.ds(at, size)
        here = kh[i, rows, :]
        fx[i, rows, :] = harmonic(kh[i - 1, rows, :], here)
        fy[i, rows, :] = harmonic(kh[i, pl.ds(at - 1, size), :], here)
        k = kv[i, rows, :]
        z = harmonic(k, up(k))
        fz[i, rows, :] = jnp.where(iota((size, NZ), 1) < NZ - 1, z, 0.0)

    def rim_faces(i, _):
        for at, size, _j in RIM_CHUNKS:
            set_faces(i, at, size)
        return 0

    lax.fori_loop(1, PLANES - 1, rim_faces, 0)
    for i in RIM_PLANES:
        for at, size, _j in OWN_CHUNKS:
            set_faces(i, at, size)
    last = PLANES - 1
    for at, size, _j in CHUNKS:
        rows = pl.ds(at, size)
        fx[last, rows, :] = harmonic(kh[last - 1, rows, :], kh[last, rows, :])

    def rim_scales(i, mask, source_low, source_high):
        set_scale(i, 8, 8, mask * inside[2], source_low, fx, fy, fz, scale, None, s1)
        set_scale(i, 144, 8, mask * inside[3], source_high, fx, fy, fz, scale, None, s1)

    def own_rims(x, _):
        rim_scales(x + HX, 1.0, ylo[NXL + x], yhi[NXL + x])
        return 0

    lax.fori_loop(0, NXL, own_rims, 0)
    for n in range(2):
        for side, i, msg in ((0, 1 + n, xlo), (1, HX + NXL + n, xhi)):
            corner = 6 + 2 * side + n
            rim_scales(i, inside[side], below[corner], above[corner])
            for at, size, _j in OWN_CHUNKS:
                source = msg[3 + n, pl.ds(at - OWN, size), :]
                set_scale(i, at, size, inside[side], source, fx, fy, fz, scale, None, s1)

    def smooth(i, _):
        for at, size, j in CHUNKS:
            smooth_chunk(s1, d, fx, fy, fz, scale, spread, i, at, size, j)
        return 0

    lax.fori_loop(HX - 1, HX + NXL + 1, smooth, 0)

    def image(x, _):
        i = x + HX
        for at, size, j in OWN_CHUNKS:
            here, total = neighbours(d, fx, fy, fz, i, at, size)
            q = centre[i, pl.ds(at, size), :] * here - total
            q_out[x, pl.ds(at - OWN, size), :] = q
            d_out[x, pl.ds(at - OWN, size), :] = here
        return 0

    lax.fori_loop(0, NXL, image, 0)
    for a in range(4):
        for j in range(4):
            rows = pl.ds(32 * j, 32)
            source = q_out[2 * a, rows, :] + q_out[2 * a + 1, rows, :]
            tiles[pl.ds(8 * (4 * a + j), 8), :] = row_group(source)
    tiles[...] = dot(tiles[...], sum_matrix())
    tile = gather_tile(
        [
            [(SOURCE, j, tiles[pl.ds(8 * (4 * a + j), 8), :]) for j in range(4)]
            for a in range(4)
        ]
    )
    tile_out[...] = tile
    low_plane, high_plane = 0, NXL - 2
    odd = inside[4] > 0.5
    far, near = jnp.where(odd, high_plane, low_plane), jnp.where(odd, low_plane, high_plane)
    for n in range(2):
        q_far[pl.ds(128 * n, 128), :] = q_out[far + n]
        q_near[pl.ds(128 * n, 128), :] = q_out[near + n]
    q_far[256:264, :] = tile
    q_near[256:264, :] = tile


INNER_CHUNKS = ((24, 24, 0), (48, 32, 1), (80, 32, 2), (112, 24, 3))
OUTER_CHUNKS = ((8, 8, -1), (16, 8, 0), (136, 8, 3), (144, 8, 4))


def inner_kernel(rhs, d0, q0, fx, fy, fz, scale, s1, d, known):
    zero_pads(s1)
    zero_pads(d)

    def plane(x, sums):
        i = x + HX
        for at, size, j in OWN_CHUNKS:
            rows = pl.ds(at - OWN, size)
            q = q0[x, rows, :]
            s1[i, pl.ds(at, size), :] = scale[i, pl.ds(at, size), :] * q
            dd = d0[x, rows, :]
            rd, dq = sums
            sums = (rd + row_group(rhs[x, rows, :] * dd), dq + row_group(dd * q))
        return sums

    zero = jnp.zeros((8, NZ), F32)
    rd, dq = lax.fori_loop(0, NXL, plane, (zero, zero))
    known[0:8, :] = rd
    known[8:16, :] = dq

    def smooth(i, _):
        for at, size, j in INNER_CHUNKS:
            smooth_chunk(s1, d, fx, fy, fz, scale, None, i, at, size, j)
        return 0

    lax.fori_loop(HX + 1, HX + NXL - 1, smooth, 0)


def second_kernel(
    rhs, d0, q0, xlo, xhi, own, below, above, coefs, fx, fy, fz, scale, centre, known,
    _s1, _d, p_out, s_out, dots, s1, d, stack, spread,
):
    mid = stack_tiles(stack, xlo[256:264, :], own[...], xhi[256:264, :])
    low = stack_tiles(stack, below[12], below[13], below[14])
    high = stack_tiles(stack, above[12], above[13], above[14])
    wide = widen(SOURCE, low, mid, high)
    spread_coarse(coarse_sweeps([coefs[k] for k in range(6)], wide), spread)

    def rims(i, _):
        s1[i, 8:16, :] = scale[i, 8:16, :] * below[i - 1]
        s1[i, 144:152, :] = scale[i, 144:152, :] * above[i - 1]
        return 0

    lax.fori_loop(1, PLANES - 1, rims, 0)
    for n in range(2):
        for i, msg in ((1 + n, xlo), (HX + NXL + n, xhi)):
            s1[i, 16:144, :] = scale[i, 16:144, :] * msg[pl.ds(128 * n, 128), :]

    for i in (HX - 1, HX, HX + NXL - 1, HX + NXL):
        for at, size, j in CHUNKS:
            smooth_chunk(s1, d, fx, fy, fz, scale, spread, i, at, size, j)

    def smooth(i, _):
        for at, size, j in OUTER_CHUNKS:
            smooth_chunk(s1, d, fx, fy, fz, scale, spread, i, at, size, j)
        for at, size, j in INNER_CHUNKS:
            rows = pl.ds(at, size)
            d[i, rows, :] = d[i, rows, :] + spread[j + 1, pl.ds((i + 5) // 2, 1), :]
        return 0

    lax.fori_loop(HX + 1, HX + NXL - 1, smooth, 0)

    def image(x, sums):
        i = x + HX
        for at, size, j in OWN_CHUNKS:
            rows = pl.ds(at - OWN, size)
            p, total = neighbours(d, fx, fy, fz, i, at, size)
            s = centre[i, pl.ds(at, size), :] * p - total
            p_out[x, rows, :] = p
            s_out[x, rows, :] = s
            r, dd, q = rhs[x, rows, :], d0[x, rows, :], q0[x, rows, :]
            pairs = ((r, p), (q, p), (dd, s), (p, s))
            sums = tuple(
                acc + row_group(u * v) for acc, (u, v) in zip(sums, pairs)
            )
        return sums

    zero = jnp.zeros((8, NZ), F32)
    sums = lax.fori_loop(0, NXL, image, (zero,) * 4)
    sums = (known[0:8, :], known[8:16, :]) + sums
    sublane, lane = iota((8, NZ), 0), iota((8, NZ), 1)
    tile = zero
    for n, acc in enumerate(sums):
        tile = jnp.where(sublane == n, jnp.sum(acc, axis=0, keepdims=True), tile)
    tile = jnp.where(sublane == lane, jnp.sum(tile, axis=1, keepdims=True), 0.0)
    dots[...] = jnp.sum(tile, axis=0, keepdims=True)


def last_kernel(parts, rhs, d0, q0, p, s, x_out, r_out):
    total = parts[0:8, :]
    for n in range(8, parts.shape[0], 8):
        total = total + parts[n : n + 8, :]
    sums = jnp.sum(total, axis=0, keepdims=True)
    rd, dq, rp, qp, ds, ps = [sums[:, n : n + 1] for n in range(6)]
    a0 = rd / dq
    rz = rd - a0 * rp - a0 * dq + a0 * a0 * qp
    ratio = rz / rd
    grow = 1.0 + ratio
    curve = grow * grow * dq - grow * a0 * (ds + qp) + a0 * a0 * ps
    a1 = rz / curve
    u = jnp.broadcast_to(a0 + a1 * grow, (8, NZ))[0:1, :]
    v = jnp.broadcast_to(a1 * a0, (8, NZ))[0:1, :]

    def plane(x, _):
        for at in range(0, NYL, 32):
            rows = pl.ds(at, 32)
            x_out[x, rows, :] = u * d0[x, rows, :] - v * p[x, rows, :]
            r_out[x, rows, :] = rhs[x, rows, :] - u * q0[x, rows, :] + v * s[x, rows, :]
        return 0

    lax.fori_loop(0, NXL, plane, 0)


VMEM = pl.BlockSpec(memory_space=pltpu.VMEM)
SMEM = pl.BlockSpec(memory_space=pltpu.SMEM)


def call(kernel, name, operands, outs, scratch, scalars=0, aliases=None):
    return pl.pallas_call(
        kernel,
        name=name,
        out_shape=[jax.ShapeDtypeStruct(s, F32) for s in outs],
        in_specs=[SMEM] * scalars + [VMEM] * (len(operands) - scalars),
        out_specs=[VMEM] * len(outs),
        scratch_shapes=[pltpu.VMEM(s, F32) for s in scratch],
        input_output_aliases=aliases or {},
        compiler_params=pltpu.CompilerParams(vmem_limit_bytes=24 * 1024 * 1024),
    )(*operands)


def swap(values, axis, first):
    pairs = []
    for i in range(first, lax.axis_size(axis) - 1, 2):
        pairs += [(i, i + 1), (i + 1, i)]
    return lax.ppermute(values, axis, pairs)


def sides(far, near, odd):
    return jnp.where(odd, near, far), jnp.where(odd, far, near)


def swap_both(to_low, to_high, axis, odd):
    far = swap(jnp.where(odd, to_high, to_low), axis, 1)
    near = swap(jnp.where(odd, to_low, to_high), axis, 0)
    return sides(far, near, odd)


def exchange(row, axes):
    count = lax.axis_size(axes)
    rows = jnp.broadcast_to(row[None], (count, 1, NZ))
    return lax.all_to_all(rows, axes, 0, 0).reshape(count, NZ)


STAGES = (("sy", "cg"), "sx")


def body(right_side, perm_class, perm_table):
    x_at, y_at = lax.axis_index(X_AXES), lax.axis_index("sy")
    x_end, y_end = lax.axis_size(X_AXES) - 1, lax.axis_size("sy") - 1
    x_odd, y_odd = x_at % 2 == 1, y_at % 2 == 1
    flags = [x_at > 0, x_at < x_end, y_at > 0, y_at < y_end, x_odd]
    inside = jnp.stack(flags).astype(F32)
    pad = ((0, 6), (0, NZ - perm_table.shape[1]))
    table = jnp.pad(perm_table, pad, constant_values=1.0)

    def packed(classes, values):
        return jnp.concatenate([classes.astype(F32), values])

    def x_planes(low):
        classes = lax.dynamic_slice_in_dim(perm_class, jnp.where(low, 0, NXL - 3), 3)
        values = lax.dynamic_slice_in_dim(right_side, jnp.where(low, 0, NXL - 2), 2)
        return packed(classes, values)

    def y_rows(at):
        return packed(perm_class[:, at : at + 8], right_side[:, at : at + 8])

    x_far = swap(x_planes(~x_odd), X_AXES, 1)
    x_near = swap(x_planes(x_odd), X_AXES, 0)
    ylo, yhi = swap_both(y_rows(0), y_rows(NYL - 8), "sy", y_odd)
    xlo, xhi = sides(x_far, x_near, x_odd)
    block, big = (NXL, NYL, NZ), (PLANES, ROWS, NZ)
    kh, kv, fz, tiles = call(
        own_kernel, "own", (table, perm_class, right_side), [big] * 3 + [(448, NZ)], []
    )
    halos = (xlo, xhi, ylo, yhi)
    (own,) = call(
        coarse_kernel, "coarse", (inside, table) + halos + (kh, tiles), [(8, NZ)],
        [(128, NZ)], 1,
    )
    kh, kv, fx, fy, scale, centre, s1 = call(
        cells_kernel, "cells", (inside, table, right_side) + halos + (kh, kv, fz),
        [big] * 7, [], 1, {7: 0, 8: 1},
    )
    left, right = swap_both(own, own, X_AXES, x_odd)

    def rim(rows):
        parts = [xlo[:3, rows], xhi[:3, rows], xlo[3:, rows], xhi[3:, rows]]
        return jnp.concatenate(parts + [left[None], own[None], right[None]])

    below, above = swap_both(rim(slice(0, 8)), rim(slice(NYL - 8, NYL)), "sy", y_odd)

    d0, q0, q_far, q_near, tile, coefs, _, _, fx, fy, fz, scale, _ = call(
        first_kernel, "first",
        (inside, table) + halos + (left, own, right, below, above, centre)
        + (kh, kv, fx, fy, fz, scale, s1),
        [block, block, (264, NZ), (264, NZ), (8, NZ), (6, 16, NZ)] + [big] * 7,
        [big, (16, NZ), (6, 16, NZ), (16 * 8, NZ)], 1,
        {12 + n: 6 + n for n in range(7)},
    )
    qlo, qhi = sides(swap(q_far, X_AXES, 1), swap(q_near, X_AXES, 0), x_odd)
    s1, d, known = call(
        inner_kernel, "inner", (right_side, d0, q0, fx, fy, fz, scale),
        [big, big, (16, NZ)], [],
    )

    def rim_q(at):
        parts = [qlo[at : at + 8][None], qlo[128 + at : 136 + at][None], q0[:, at : at + 8]]
        parts += [qhi[at : at + 8][None], qhi[128 + at : 136 + at][None]]
        return jnp.concatenate(parts + [qlo[256:][None], tile[None], qhi[256:][None]])

    below, above = swap_both(rim_q(0), rim_q(NYL - 8), "sy", y_odd)
    p, s, dots, _, _ = call(
        second_kernel, "second",
        (right_side, d0, q0, qlo, qhi, tile, below, above, coefs, fx, fy, fz, scale, centre)
        + (known, s1, d),
        [block, block, (1, NZ), big, big], [(16, NZ), (6, 16, NZ)], 0, {15: 3, 16: 4},
    )
    for axes in STAGES[:-1]:
        dots = exchange(dots, axes).sum(0, keepdims=True)
    dots = exchange(dots, STAGES[-1])
    return tuple(
        call(last_kernel, "last", (dots, right_side, d0, q0, p, s), [block, block], [])
    )


def solution(mesh):
    cells = P(X_AXES, "sy", None)
    return jax.shard_map(
        body,
        mesh=mesh,
        in_specs=(cells, cells, P()),
        out_specs=(cells, cells),
        check_vma=False,
    )
```

```python
import jax
import jax.numpy as jnp
from jax import lax
from jax.experimental import pallas as pl
from jax.experimental.pallas import tpu as pltpu
from jax.sharding import PartitionSpec as P

F32 = jnp.float32
W = 2.0 / 3.0
X_AXES = ("sx", "cg")
SWEEPS = 3

NXL, NYL, NZ = 8, 128, 128
HX = 3
PLANES = NXL + 2 * HX
ROWS = 160
OWN = 16
CHUNKS = ((8, 8, -1), (16, 32, 0), (48, 32, 1), (80, 32, 2), (112, 32, 3), (144, 8, 4))
OWN_CHUNKS = CHUNKS[1:5]
X_LOW, X_HIGH, Y_LOW, Y_HIGH, Z_UP, SOURCE = range(6)


OUTSIDE = 1e-30


def harmonic(a, b):
    return pl.reciprocal(a + b)


def up(v):
    return pltpu.roll(v, NZ - 1, 1)


def down(v):
    return pltpu.roll(v, 1, 1)


def look_up(row, index):
    table = jnp.broadcast_to(row, index.shape)
    return jnp.take_along_axis(table, index, axis=1, mode="promise_in_bounds")


def iota(shape, dim):
    return lax.broadcasted_iota(jnp.int32, shape, dim)


def dot(a, b):
    return jnp.dot(a, b, precision=lax.Precision.HIGHEST, preferred_element_type=F32)


def sum_matrix():
    return jnp.where(iota((NZ, NZ), 0) // 32 == iota((NZ, NZ), 1) % 4, 1.0, 0.0).astype(F32)


def top_matrix():
    lane, col = iota((NZ, NZ), 0), iota((NZ, NZ), 1) % 4
    return jnp.where((lane == 32 * col + 31) & (col < 3), 1.0, 0.0).astype(F32)


def row_group(values):
    return (values[0:8] + values[8:16]) + (values[16:24] + values[24:32])


def gather_tile(pieces):
    group = iota((8, NZ), 1) // 4
    sublane = iota((8, NZ), 0)
    tile = jnp.zeros((8, NZ), F32)
    for a, parts in enumerate(pieces):
        acc = jnp.zeros((8, NZ), F32)
        for field, j, part in parts:
            acc = jnp.where(group == 4 * field + j, part, acc)
        tile = jnp.where(sublane == a, jnp.sum(acc, axis=0, keepdims=True), tile)
    return tile


def own_kernel(table, cls, rhs, kh, kv, fz, tiles):
    khrow, kvrow = 0.5 / table[0:1, :], 0.5 / table[1:2, :]

    def plane(x, _):
        i = x + HX
        for at, size, _j in OWN_CHUNKS:
            rows = pl.ds(at, size)
            index = cls[x, pl.ds(at - OWN, size), :]
            kh[i, rows, :] = look_up(khrow, index)
            k = look_up(kvrow, index)
            kv[i, rows, :] = k
            z = harmonic(k, up(k))
            fz[i, rows, :] = jnp.where(iota((size, NZ), 1) < NZ - 1, z, 0.0)
        return 0

    lax.fori_loop(0, NXL, plane, 0, unroll=True)
    first = iota((8, NZ), 0) == 0
    for f in range(1, 4):
        for j in range(4):
            rows = pl.ds(OWN + 32 * j, 32)
            face = harmonic(kh[2 * f + 2, rows, :], kh[2 * f + 3, rows, :])
            tiles[pl.ds(8 * (4 * (f - 1) + j), 8), :] = row_group(face)
    for a in range(4):
        low, high = 2 * a + HX, 2 * a + HX + 1
        for j in range(1, 4):
            here, under = pl.ds(OWN + 32 * j, 8), pl.ds(OWN + 32 * j - 1, 8)
            total = harmonic(kh[low, under, :], kh[low, here, :])
            total = total + harmonic(kh[high, under, :], kh[high, here, :])
            tiles[pl.ds(8 * (11 + 3 * a + j), 8), :] = jnp.where(first, total, 0.0)
        for j in range(4):
            rows = pl.ds(32 * j, 32)
            source = rhs[2 * a, rows, :] + rhs[2 * a + 1, rows, :]
            tiles[pl.ds(8 * (24 + 4 * a + j), 8), :] = row_group(source)
            rows = pl.ds(OWN + 32 * j, 32)
            upper = fz[low, rows, :] + fz[high, rows, :]
            tiles[pl.ds(8 * (40 + 4 * a + j), 8), :] = row_group(upper)
    tiles[0:320, :] = dot(tiles[0:320, :], sum_matrix())
    tiles[320:448, :] = dot(tiles[320:448, :], top_matrix())


def coarse_kernel(inside, table, xlo, xhi, ylo, yhi, kh, tiles, out, rims):
    khrow = 0.5 / table[0:1, :]

    def rim(classes, side):
        values = look_up(khrow, classes.astype(jnp.int32))
        return jnp.where(inside[side] > 0.5, values, OUTSIDE)

    first = iota((8, NZ), 0) == 0
    for j in range(4):
        rows, own = pl.ds(32 * j, 32), pl.ds(OWN + 32 * j, 32)
        face = harmonic(rim(xlo[2, rows, :], 0), kh[HX, own, :])
        rims[pl.ds(8 * j, 8), :] = row_group(face)
        face = harmonic(kh[HX + NXL - 1, own, :], rim(xhi[0, rows, :], 1))
        rims[pl.ds(8 * (4 + j), 8), :] = row_group(face)
    for a in range(4):
        low = high = jnp.zeros((8, NZ), F32)
        for x in (2 * a, 2 * a + 1):
            i = x + HX
            under = pltpu.roll(rim(ylo[x], 2), 1, 0)
            low = low + harmonic(under, kh[i, OWN : OWN + 8, :])
            high = high + harmonic(kh[i, 143:151, :], rim(yhi[x], 3))
        rims[pl.ds(8 * (8 + a), 8), :] = jnp.where(first, low, 0.0)
        rims[pl.ds(8 * (12 + a), 8), :] = jnp.where(first, high, 0.0)
    rims[...] = dot(rims[...], sum_matrix())

    def inner(t):
        return tiles[pl.ds(8 * t, 8), :]

    def outer(t):
        return rims[pl.ds(8 * t, 8), :]

    def x_face(f, j):
        return outer(f + j) if f in (0, 4) else inner(4 * (f - 1) + j)

    def y_face(a, j):
        return outer(8 + a + j) if j in (0, 4) else inner(11 + 3 * a + j)

    pieces = []
    for a in range(4):
        parts = []
        for j in range(4):
            parts += [
                (X_LOW, j, x_face(a, j)),
                (X_HIGH, j, x_face(a + 1, j)),
                (Y_LOW, j, y_face(a, j)),
                (Y_HIGH, j, y_face(a, j + 1)),
                (Z_UP, j, inner(40 + 4 * a + j)),
                (SOURCE, j, inner(24 + 4 * a + j)),
            ]
        pieces.append(parts)
    out[...] = gather_tile(pieces)


def stack_tiles(buf, left, own, right):
    buf[0:4, :] = left[0:4, :]
    buf[4:8, :] = own[0:4, :]
    buf[8:12, :] = right[0:4, :]
    buf[12:16, :] = jnp.zeros((4, NZ), F32)
    return buf[...]


def widen(field, below, own, above):
    lane = iota((16, NZ), 1)

    def placed(v, at):
        shift = (at - 16 * field) % NZ
        return pltpu.roll(v, shift, 1) if shift else v

    wide = jnp.where(lane < 16, placed(below, 0), placed(own, 16))
    wide = jnp.where(lane < 32, wide, placed(above, 32))
    return jnp.where(lane < 48, wide, 0.0)


def coarse_sweeps(coefs, source):
    x_low, x_high, y_low, y_high, z_up, scale = coefs
    start = scale * source
    c = start
    for _ in range(SWEEPS):
        beside = x_low * pltpu.roll(c, 1, 0) + x_high * pltpu.roll(c, 15, 0)
        beside = beside + y_low * pltpu.roll(c, 4, 1) + y_high * pltpu.roll(c, NZ - 4, 1)
        beside = beside + z_up * up(c) + down(z_up * c)
        c = (1.0 - W) * c + (start + scale * beside)
    return c


def spread_coarse(c, spread):
    for k in range(6):
        lane = iota((NZ, NZ), 1)
        pick = jnp.where(iota((NZ, NZ), 0) == 4 * (k + 3) + lane // 32, 1.0, 0.0)
        spread[k] = dot(c, pick.astype(F32))


def neighbours(v, fx, fy, fz, i, at, size):
    here = v[i, pl.ds(at, size), :]
    total = fx[i, pl.ds(at, size), :] * v[i - 1, pl.ds(at, size), :]
    total = total + fx[i + 1, pl.ds(at, size), :] * v[i + 1, pl.ds(at, size), :]
    total = total + fy[i, pl.ds(at, size), :] * v[i, pl.ds(at - 1, size), :]
    total = total + fy[i, pl.ds(at + 1, size), :] * v[i, pl.ds(at + 1, size), :]
    z = fz[i, pl.ds(at, size), :]
    return here, total + z * up(here) + down(z * here)


def smooth_chunk(s1, d, fx, fy, fz, scale, spread, i, at, size, j):
    here, total = neighbours(s1, fx, fy, fz, i, at, size)
    value = (2.0 - W) * here + scale[i, pl.ds(at, size), :] * total
    if spread is not None:
        value = value + spread[j + 1, pl.ds((i + 5) // 2, 1), :]
    d[i, pl.ds(at, size), :] = value


def zero_pads(v):
    def plane(i, _):
        v[i, 0:8, :] = jnp.zeros((8, NZ), F32)
        v[i, ROWS - 8 : ROWS, :] = jnp.zeros((8, NZ), F32)
        return 0

    lax.fori_loop(0, PLANES, plane, 0, unroll=True)


def looked_up(inside, table, kh, kv, i, at, size, classes, *sides):
    index = classes.astype(jnp.int32)
    values = look_up(0.5 / table[0:1, :], index)
    for side in sides:
        values = jnp.where(inside[side] > 0.5, values, OUTSIDE)
    kh[i, pl.ds(at, size), :] = values
    if 0 < i < PLANES - 1 if isinstance(i, int) else True:
        kv[i, pl.ds(at, size), :] = look_up(0.5 / table[1:2, :], index)


def set_scale(i, at, size, mask, source, fx, fy, fz, scale, centre, s1):
    rows = pl.ds(at, size)
    z = fz[i, rows, :]
    total = fx[i, rows, :] + fx[i + 1, rows, :]
    total = total + fy[i, rows, :] + fy[i, pl.ds(at + 1, size), :] + (z + down(z))
    inverse = (W * mask) * pl.reciprocal(total)
    scale[i, rows, :] = inverse
    s1[i, rows, :] = inverse * source
    if centre is not None:
        centre[i, rows, :] = total


def cells_kernel(
    inside, table, rhs, xlo, xhi, ylo, yhi, _kh, _kv, fz,
    kh, kv, fx, fy, scale, centre, s1,
):
    def rims(x, _):
        looked_up(inside, table, kh, kv, x + HX, 8, 8, ylo[x], 2)
        looked_up(inside, table, kh, kv, x + HX, 144, 8, yhi[x], 3)
        return 0

    lax.fori_loop(0, NXL, rims, 0, unroll=True)
    for n in range(3):
        for side, base, msg in ((0, 0, xlo), (1, HX + NXL, xhi)):
            looked_up(inside, table, kh, kv, base + n, OWN, NYL, msg[n], side)

    def faces(i, _):
        for at, size, j in OWN_CHUNKS:
            rows = pl.ds(at, size)
            here = kh[i, rows, :]
            fx[i, rows, :] = harmonic(kh[i - 1, rows, :], here)
            fy[i, rows, :] = harmonic(kh[i, pl.ds(at - 1, size), :], here)
        fy[i, 144:152, :] = harmonic(kh[i, 143:151, :], kh[i, 144:152, :])
        return 0

    lax.fori_loop(HX, HX + NXL, faces, 0, unroll=True)
    end = HX + NXL
    fx[end, 16:144, :] = harmonic(kh[end - 1, 16:144, :], kh[end, 16:144, :])

    def scales(x, _):
        for at, size, j in OWN_CHUNKS:
            source = rhs[x, pl.ds(at - OWN, size), :]
            set_scale(x + HX, at, size, 1.0, source, fx, fy, fz, scale, centre, s1)
        return 0

    lax.fori_loop(0, NXL, scales, 0, unroll=True)


RIM_PLANES = (1, 2, HX + NXL, HX + NXL + 1)
RIM_CHUNKS = (CHUNKS[0], CHUNKS[5])


def first_kernel(
    inside, table, xlo, xhi, ylo, yhi, left, own, right, below, above, centre,
    _kh, _kv, _fx, _fy, _fz, _scale, _s1,
    d_out, q_out, q_far, q_near, tile_out, coefs_out, kh, kv, fx, fy, fz, scale, s1,
    d, stack, spread, tiles,
):
    for n in range(3):
        for side, i in ((0, n), (1, HX + NXL + n)):
            corner = 3 * side + n
            looked_up(inside, table, kh, kv, i, 8, 8, below[corner], side, 2)
            looked_up(inside, table, kh, kv, i, 144, 8, above[corner], side, 3)

    def pads(i, _):
        ones = jnp.ones((8, NZ), F32)
        kh[i, 0:8, :] = ones
        kh[i, ROWS - 8 : ROWS, :] = ones
        fy[i, ROWS - 8 : ROWS, :] = ones
        return 0

    lax.fori_loop(0, PLANES, pads, 0, unroll=True)
    zero_pads(s1)
    zero_pads(d)

    mid = stack_tiles(stack, left, own, right)
    low = stack_tiles(stack, below[10], below[11], below[12])
    high = stack_tiles(stack, above[10], above[11], above[12])
    wide = [widen(k, low, mid, high) for k in range(6)]
    total = wide[0] + wide[1] + wide[2] + wide[3] + wide[4] + down(wide[4])
    valid = total > 0.0
    wide_scale = jnp.where(valid, W / jnp.where(valid, total, 1.0), 0.0)
    coefs = wide[:5] + [wide_scale]
    for k in range(6):
        coefs_out[k] = coefs[k]
    spread_coarse(coarse_sweeps(coefs, wide[SOURCE]), spread)

    def set_faces(i, at, size):
        rows = pl.ds(at, size)
        here = kh[i, rows, :]
        fx[i, rows, :] = harmonic(kh[i - 1, rows, :], here)
        fy[i, rows, :] = harmonic(kh[i, pl.ds(at - 1, size), :], here)
        k = kv[i, rows, :]
        z = harmonic(k, up(k))
        fz[i, rows, :] = jnp.where(iota((size, NZ), 1) < NZ - 1, z, 0.0)

    def rim_faces(i, _):
        for at, size, _j in RIM_CHUNKS:
            set_faces(i, at, size)
        return 0

    lax.fori_loop(1, PLANES - 1, rim_faces, 0, unroll=True)
    for i in RIM_PLANES:
        for at, size, _j in OWN_CHUNKS:
            set_faces(i, at, size)
    last = PLANES - 1
    for at, size, _j in CHUNKS:
        rows = pl.ds(at, size)
        fx[last, rows, :] = harmonic(kh[last - 1, rows, :], kh[last, rows, :])

    def rim_scales(i, mask, source_low, source_high):
        set_scale(i, 8, 8, mask * inside[2], source_low, fx, fy, fz, scale, None, s1)
        set_scale(i, 144, 8, mask * inside[3], source_high, fx, fy, fz, scale, None, s1)

    def own_rims(x, _):
        rim_scales(x + HX, 1.0, ylo[NXL + x], yhi[NXL + x])
        return 0

    lax.fori_loop(0, NXL, own_rims, 0, unroll=True)
    for n in range(2):
        for side, i, msg in ((0, 1 + n, xlo), (1, HX + NXL + n, xhi)):
            corner = 6 + 2 * side + n
            rim_scales(i, inside[side], below[corner], above[corner])
            for at, size, _j in OWN_CHUNKS:
                source = msg[3 + n, pl.ds(at - OWN, size), :]
                set_scale(i, at, size, inside[side], source, fx, fy, fz, scale, None, s1)

    def smooth(i, _):
        for at, size, j in CHUNKS:
            smooth_chunk(s1, d, fx, fy, fz, scale, spread, i, at, size, j)
        return 0

    lax.fori_loop(HX - 1, HX + NXL + 1, smooth, 0, unroll=True)

    def image(x, _):
        i = x + HX
        for at, size, j in OWN_CHUNKS:
            here, total = neighbours(d, fx, fy, fz, i, at, size)
            q = centre[i, pl.ds(at, size), :] * here - total
            q_out[x, pl.ds(at - OWN, size), :] = q
            d_out[x, pl.ds(at - OWN, size), :] = here
        return 0

    lax.fori_loop(0, NXL, image, 0, unroll=True)
    for a in range(4):
        for j in range(4):
            rows = pl.ds(32 * j, 32)
            source = q_out[2 * a, rows, :] + q_out[2 * a + 1, rows, :]
            tiles[pl.ds(8 * (4 * a + j), 8), :] = row_group(source)
    tiles[...] = dot(tiles[...], sum_matrix())
    tile = gather_tile(
        [
            [(SOURCE, j, tiles[pl.ds(8 * (4 * a + j), 8), :]) for j in range(4)]
            for a in range(4)
        ]
    )
    tile_out[...] = tile
    low_plane, high_plane = 0, NXL - 2
    odd = inside[4] > 0.5
    far, near = jnp.where(odd, high_plane, low_plane), jnp.where(odd, low_plane, high_plane)
    for n in range(2):
        q_far[pl.ds(128 * n, 128), :] = q_out[far + n]
        q_near[pl.ds(128 * n, 128), :] = q_out[near + n]
    q_far[256:264, :] = tile
    q_near[256:264, :] = tile


INNER_CHUNKS = ((24, 24, 0), (48, 32, 1), (80, 32, 2), (112, 24, 3))
OUTER_CHUNKS = ((8, 8, -1), (16, 8, 0), (136, 8, 3), (144, 8, 4))


def inner_kernel(rhs, d0, q0, fx, fy, fz, scale, s1, d, known):
    zero_pads(s1)
    zero_pads(d)

    def plane(x, sums):
        i = x + HX
        for at, size, j in OWN_CHUNKS:
            rows = pl.ds(at - OWN, size)
            q = q0[x, rows, :]
            s1[i, pl.ds(at, size), :] = scale[i, pl.ds(at, size), :] * q
            dd = d0[x, rows, :]
            rd, dq = sums
            sums = (rd + row_group(rhs[x, rows, :] * dd), dq + row_group(dd * q))
        return sums

    zero = jnp.zeros((8, NZ), F32)
    rd, dq = lax.fori_loop(0, NXL, plane, (zero, zero), unroll=True)
    known[0:8, :] = rd
    known[8:16, :] = dq

    def smooth(i, _):
        for at, size, j in INNER_CHUNKS:
            smooth_chunk(s1, d, fx, fy, fz, scale, None, i, at, size, j)
        return 0

    lax.fori_loop(HX + 1, HX + NXL - 1, smooth, 0, unroll=True)


def second_kernel(
    rhs, d0, q0, xlo, xhi, own, below, above, coefs, fx, fy, fz, scale, centre, known,
    _s1, _d, p_out, s_out, dots, s1, d, stack, spread,
):
    mid = stack_tiles(stack, xlo[256:264, :], own[...], xhi[256:264, :])
    low = stack_tiles(stack, below[12], below[13], below[14])
    high = stack_tiles(stack, above[12], above[13], above[14])
    wide = widen(SOURCE, low, mid, high)
    spread_coarse(coarse_sweeps([coefs[k] for k in range(6)], wide), spread)

    def rims(i, _):
        s1[i, 8:16, :] = scale[i, 8:16, :] * below[i - 1]
        s1[i, 144:152, :] = scale[i, 144:152, :] * above[i - 1]
        return 0

    lax.fori_loop(1, PLANES - 1, rims, 0, unroll=True)
    for n in range(2):
        for i, msg in ((1 + n, xlo), (HX + NXL + n, xhi)):
            s1[i, 16:144, :] = scale[i, 16:144, :] * msg[pl.ds(128 * n, 128), :]

    for i in (HX - 1, HX, HX + NXL - 1, HX + NXL):
        for at, size, j in CHUNKS:
            smooth_chunk(s1, d, fx, fy, fz, scale, spread, i, at, size, j)

    def smooth(i, _):
        for at, size, j in OUTER_CHUNKS:
            smooth_chunk(s1, d, fx, fy, fz, scale, spread, i, at, size, j)
        for at, size, j in INNER_CHUNKS:
            rows = pl.ds(at, size)
            d[i, rows, :] = d[i, rows, :] + spread[j + 1, pl.ds((i + 5) // 2, 1), :]
        return 0

    lax.fori_loop(HX + 1, HX + NXL - 1, smooth, 0, unroll=True)

    def image(x, sums):
        i = x + HX
        for at, size, j in OWN_CHUNKS:
            rows = pl.ds(at - OWN, size)
            p, total = neighbours(d, fx, fy, fz, i, at, size)
            s = centre[i, pl.ds(at, size), :] * p - total
            p_out[x, rows, :] = p
            s_out[x, rows, :] = s
            r, dd, q = rhs[x, rows, :], d0[x, rows, :], q0[x, rows, :]
            pairs = ((r, p), (q, p), (dd, s), (p, s))
            sums = tuple(
                acc + row_group(u * v) for acc, (u, v) in zip(sums, pairs)
            )
        return sums

    zero = jnp.zeros((8, NZ), F32)
    sums = lax.fori_loop(0, NXL, image, (zero,) * 4, unroll=True)
    sums = (known[0:8, :], known[8:16, :]) + sums
    sublane, lane = iota((8, NZ), 0), iota((8, NZ), 1)
    tile = zero
    for n, acc in enumerate(sums):
        tile = jnp.where(sublane == n, jnp.sum(acc, axis=0, keepdims=True), tile)
    tile = jnp.where(sublane == lane, jnp.sum(tile, axis=1, keepdims=True), 0.0)
    dots[...] = jnp.sum(tile, axis=0, keepdims=True)


def last_kernel(parts, rhs, d0, q0, p, s, x_out, r_out):
    total = parts[0:8, :]
    for n in range(8, parts.shape[0], 8):
        total = total + parts[n : n + 8, :]
    sums = jnp.sum(total, axis=0, keepdims=True)
    rd, dq, rp, qp, ds, ps = [sums[:, n : n + 1] for n in range(6)]
    a0 = rd / dq
    rz = rd - a0 * rp - a0 * dq + a0 * a0 * qp
    ratio = rz / rd
    grow = 1.0 + ratio
    curve = grow * grow * dq - grow * a0 * (ds + qp) + a0 * a0 * ps
    a1 = rz / curve
    u = jnp.broadcast_to(a0 + a1 * grow, (8, NZ))[0:1, :]
    v = jnp.broadcast_to(a1 * a0, (8, NZ))[0:1, :]

    def plane(x, _):
        for at in range(0, NYL, 32):
            rows = pl.ds(at, 32)
            x_out[x, rows, :] = u * d0[x, rows, :] - v * p[x, rows, :]
            r_out[x, rows, :] = rhs[x, rows, :] - u * q0[x, rows, :] + v * s[x, rows, :]
        return 0

    lax.fori_loop(0, NXL, plane, 0, unroll=True)


VMEM = pl.BlockSpec(memory_space=pltpu.VMEM)
SMEM = pl.BlockSpec(memory_space=pltpu.SMEM)


def call(kernel, name, operands, outs, scratch, scalars=0, aliases=None):
    return pl.pallas_call(
        kernel,
        name=name,
        out_shape=[jax.ShapeDtypeStruct(s, F32) for s in outs],
        in_specs=[SMEM] * scalars + [VMEM] * (len(operands) - scalars),
        out_specs=[VMEM] * len(outs),
        scratch_shapes=[pltpu.VMEM(s, F32) for s in scratch],
        input_output_aliases=aliases or {},
        compiler_params=pltpu.CompilerParams(vmem_limit_bytes=24 * 1024 * 1024),
    )(*operands)


def swap(values, axis, first):
    pairs = []
    for i in range(first, lax.axis_size(axis) - 1, 2):
        pairs += [(i, i + 1), (i + 1, i)]
    return lax.ppermute(values, axis, pairs)


def sides(far, near, odd):
    return jnp.where(odd, near, far), jnp.where(odd, far, near)


def swap_both(to_low, to_high, axis, odd):
    far = swap(jnp.where(odd, to_high, to_low), axis, 1)
    near = swap(jnp.where(odd, to_low, to_high), axis, 0)
    return sides(far, near, odd)


def exchange(row, axes):
    count = lax.axis_size(axes)
    rows = jnp.broadcast_to(row[None], (count, 1, NZ))
    return lax.all_to_all(rows, axes, 0, 0).reshape(count, NZ)


STAGES = (("sy", "cg"), "sx")


def body(right_side, perm_class, perm_table):
    x_at, y_at = lax.axis_index(X_AXES), lax.axis_index("sy")
    x_end, y_end = lax.axis_size(X_AXES) - 1, lax.axis_size("sy") - 1
    x_odd, y_odd = x_at % 2 == 1, y_at % 2 == 1
    flags = [x_at > 0, x_at < x_end, y_at > 0, y_at < y_end, x_odd]
    inside = jnp.stack(flags).astype(F32)
    pad = ((0, 6), (0, NZ - perm_table.shape[1]))
    table = jnp.pad(perm_table, pad, constant_values=1.0)

    def packed(classes, values):
        return jnp.concatenate([classes.astype(F32), values])

    def x_planes(low):
        classes = lax.dynamic_slice_in_dim(perm_class, jnp.where(low, 0, NXL - 3), 3)
        values = lax.dynamic_slice_in_dim(right_side, jnp.where(low, 0, NXL - 2), 2)
        return packed(classes, values)

    def y_rows(at):
        return packed(perm_class[:, at : at + 8], right_side[:, at : at + 8])

    x_far = swap(x_planes(~x_odd), X_AXES, 1)
    x_near = swap(x_planes(x_odd), X_AXES, 0)
    ylo, yhi = swap_both(y_rows(0), y_rows(NYL - 8), "sy", y_odd)
    xlo, xhi = sides(x_far, x_near, x_odd)
    block, big = (NXL, NYL, NZ), (PLANES, ROWS, NZ)
    kh, kv, fz, tiles = call(
        own_kernel, "own", (table, perm_class, right_side), [big] * 3 + [(448, NZ)], []
    )
    halos = (xlo, xhi, ylo, yhi)
    (own,) = call(
        coarse_kernel, "coarse", (inside, table) + halos + (kh, tiles), [(8, NZ)],
        [(128, NZ)], 1,
    )
    kh, kv, fx, fy, scale, centre, s1 = call(
        cells_kernel, "cells", (inside, table, right_side) + halos + (kh, kv, fz),
        [big] * 7, [], 1, {7: 0, 8: 1},
    )
    left, right = swap_both(own, own, X_AXES, x_odd)

    def rim(rows):
        parts = [xlo[:3, rows], xhi[:3, rows], xlo[3:, rows], xhi[3:, rows]]
        return jnp.concatenate(parts + [left[None], own[None], right[None]])

    below, above = swap_both(rim(slice(0, 8)), rim(slice(NYL - 8, NYL)), "sy", y_odd)

    d0, q0, q_far, q_near, tile, coefs, _, _, fx, fy, fz, scale, _ = call(
        first_kernel, "first",
        (inside, table) + halos + (left, own, right, below, above, centre)
        + (kh, kv, fx, fy, fz, scale, s1),
        [block, block, (264, NZ), (264, NZ), (8, NZ), (6, 16, NZ)] + [big] * 7,
        [big, (16, NZ), (6, 16, NZ), (16 * 8, NZ)], 1,
        {12 + n: 6 + n for n in range(7)},
    )
    qlo, qhi = sides(swap(q_far, X_AXES, 1), swap(q_near, X_AXES, 0), x_odd)
    s1, d, known = call(
        inner_kernel, "inner", (right_side, d0, q0, fx, fy, fz, scale),
        [big, big, (16, NZ)], [],
    )

    def rim_q(at):
        parts = [qlo[at : at + 8][None], qlo[128 + at : 136 + at][None], q0[:, at : at + 8]]
        parts += [qhi[at : at + 8][None], qhi[128 + at : 136 + at][None]]
        return jnp.concatenate(parts + [qlo[256:][None], tile[None], qhi[256:][None]])

    below, above = swap_both(rim_q(0), rim_q(NYL - 8), "sy", y_odd)
    p, s, dots, _, _ = call(
        second_kernel, "second",
        (right_side, d0, q0, qlo, qhi, tile, below, above, coefs, fx, fy, fz, scale, centre)
        + (known, s1, d),
        [block, block, (1, NZ), big, big], [(16, NZ), (6, 16, NZ)], 0, {15: 3, 16: 4},
    )
    for axes in STAGES[:-1]:
        dots = exchange(dots, axes).sum(0, keepdims=True)
    dots = exchange(dots, STAGES[-1])
    return tuple(
        call(last_kernel, "last", (dots, right_side, d0, q0, p, s), [block, block], [])
    )


def solution(mesh):
    cells = P(X_AXES, "sy", None)
    return jax.shard_map(
        body,
        mesh=mesh,
        in_specs=(cells, cells, P()),
        out_specs=(cells, cells),
        check_vma=False,
    )
```

```python
import jax
import jax.numpy as jnp
from jax import lax
from jax.experimental import pallas as pl
from jax.experimental.pallas import tpu as pltpu
from jax.sharding import PartitionSpec as P

F32 = jnp.float32
W = 2.0 / 3.0
X_AXES = ("sx", "cg")
SWEEPS = 3

NXL, NYL, NZ = 8, 128, 128
HX = 3
PLANES = NXL + 2 * HX
ROWS = 160
OWN = 16
CHUNKS = ((8, 8, -1), (16, 32, 0), (48, 32, 1), (80, 32, 2), (112, 32, 3), (144, 8, 4))
OWN_CHUNKS = CHUNKS[1:5]
X_LOW, X_HIGH, Y_LOW, Y_HIGH, Z_UP, SOURCE = range(6)


OUTSIDE = 1e-30


def harmonic(a, b):
    return pl.reciprocal(a + b)


def up(v):
    return pltpu.roll(v, NZ - 1, 1)


def down(v):
    return pltpu.roll(v, 1, 1)


def look_up(row, index):
    table = jnp.broadcast_to(row, index.shape)
    return jnp.take_along_axis(table, index, axis=1, mode="promise_in_bounds")


def iota(shape, dim):
    return lax.broadcasted_iota(jnp.int32, shape, dim)


def dot(a, b):
    return jnp.dot(a, b, precision=lax.Precision.HIGHEST, preferred_element_type=F32)


def sum_matrix():
    return jnp.where(iota((NZ, NZ), 0) // 32 == iota((NZ, NZ), 1) % 4, 1.0, 0.0).astype(F32)


def top_matrix():
    lane, col = iota((NZ, NZ), 0), iota((NZ, NZ), 1) % 4
    return jnp.where((lane == 32 * col + 31) & (col < 3), 1.0, 0.0).astype(F32)


def row_group(values):
    return (values[0:8] + values[8:16]) + (values[16:24] + values[24:32])


def gather_tile(pieces):
    group = iota((8, NZ), 1) // 4
    sublane = iota((8, NZ), 0)
    tile = jnp.zeros((8, NZ), F32)
    for a, parts in enumerate(pieces):
        acc = jnp.zeros((8, NZ), F32)
        for field, j, part in parts:
            acc = jnp.where(group == 4 * field + j, part, acc)
        tile = jnp.where(sublane == a, jnp.sum(acc, axis=0, keepdims=True), tile)
    return tile


def own_kernel(table, cls, rhs, kh, kv, fz, tiles):
    khrow, kvrow = 0.5 / table[0:1, :], 0.5 / table[1:2, :]

    def plane(x, _):
        i = x + HX
        for at, size, _j in OWN_CHUNKS:
            rows = pl.ds(at, size)
            index = cls[x, pl.ds(at - OWN, size), :]
            kh[i, rows, :] = look_up(khrow, index)
            k = look_up(kvrow, index)
            kv[i, rows, :] = k
            z = harmonic(k, up(k))
            fz[i, rows, :] = jnp.where(iota((size, NZ), 1) < NZ - 1, z, 0.0)
        return 0

    lax.fori_loop(0, NXL, plane, 0, unroll=True)
    first = iota((8, NZ), 0) == 0
    for f in range(1, 4):
        for j in range(4):
            rows = pl.ds(OWN + 32 * j, 32)
            face = harmonic(kh[2 * f + 2, rows, :], kh[2 * f + 3, rows, :])
            tiles[pl.ds(8 * (4 * (f - 1) + j), 8), :] = row_group(face)
    for a in range(4):
        low, high = 2 * a + HX, 2 * a + HX + 1
        for j in range(1, 4):
            here, under = pl.ds(OWN + 32 * j, 8), pl.ds(OWN + 32 * j - 1, 8)
            total = harmonic(kh[low, under, :], kh[low, here, :])
            total = total + harmonic(kh[high, under, :], kh[high, here, :])
            tiles[pl.ds(8 * (11 + 3 * a + j), 8), :] = jnp.where(first, total, 0.0)
        for j in range(4):
            rows = pl.ds(32 * j, 32)
            source = rhs[2 * a, rows, :] + rhs[2 * a + 1, rows, :]
            tiles[pl.ds(8 * (24 + 4 * a + j), 8), :] = row_group(source)
            rows = pl.ds(OWN + 32 * j, 32)
            upper = fz[low, rows, :] + fz[high, rows, :]
            tiles[pl.ds(8 * (40 + 4 * a + j), 8), :] = row_group(upper)
    tiles[0:320, :] = dot(tiles[0:320, :], sum_matrix())
    tiles[320:448, :] = dot(tiles[320:448, :], top_matrix())


def coarse_kernel(inside, table, xlo, xhi, ylo, yhi, kh, tiles, out, rims):
    khrow = 0.5 / table[0:1, :]

    def rim(classes, side):
        values = look_up(khrow, classes.astype(jnp.int32))
        return jnp.where(inside[side] > 0.5, values, OUTSIDE)

    first = iota((8, NZ), 0) == 0
    for j in range(4):
        rows, own = pl.ds(32 * j, 32), pl.ds(OWN + 32 * j, 32)
        face = harmonic(rim(xlo[2, rows, :], 0), kh[HX, own, :])
        rims[pl.ds(8 * j, 8), :] = row_group(face)
        face = harmonic(kh[HX + NXL - 1, own, :], rim(xhi[0, rows, :], 1))
        rims[pl.ds(8 * (4 + j), 8), :] = row_group(face)
    for a in range(4):
        low = high = jnp.zeros((8, NZ), F32)
        for x in (2 * a, 2 * a + 1):
            i = x + HX
            under = pltpu.roll(rim(ylo[x], 2), 1, 0)
            low = low + harmonic(under, kh[i, OWN : OWN + 8, :])
            high = high + harmonic(kh[i, 143:151, :], rim(yhi[x], 3))
        rims[pl.ds(8 * (8 + a), 8), :] = jnp.where(first, low, 0.0)
        rims[pl.ds(8 * (12 + a), 8), :] = jnp.where(first, high, 0.0)
    rims[...] = dot(rims[...], sum_matrix())

    def inner(t):
        return tiles[pl.ds(8 * t, 8), :]

    def outer(t):
        return rims[pl.ds(8 * t, 8), :]

    def x_face(f, j):
        return outer(f + j) if f in (0, 4) else inner(4 * (f - 1) + j)

    def y_face(a, j):
        return outer(8 + a + j) if j in (0, 4) else inner(11 + 3 * a + j)

    pieces = []
    for a in range(4):
        parts = []
        for j in range(4):
            parts += [
                (X_LOW, j, x_face(a, j)),
                (X_HIGH, j, x_face(a + 1, j)),
                (Y_LOW, j, y_face(a, j)),
                (Y_HIGH, j, y_face(a, j + 1)),
                (Z_UP, j, inner(40 + 4 * a + j)),
                (SOURCE, j, inner(24 + 4 * a + j)),
            ]
        pieces.append(parts)
    out[...] = gather_tile(pieces)


def stack_tiles(buf, left, own, right):
    buf[0:4, :] = left[0:4, :]
    buf[4:8, :] = own[0:4, :]
    buf[8:12, :] = right[0:4, :]
    buf[12:16, :] = jnp.zeros((4, NZ), F32)
    return buf[...]


def widen(field, below, own, above):
    lane = iota((16, NZ), 1)

    def placed(v, at):
        shift = (at - 16 * field) % NZ
        return pltpu.roll(v, shift, 1) if shift else v

    wide = jnp.where(lane < 16, placed(below, 0), placed(own, 16))
    wide = jnp.where(lane < 32, wide, placed(above, 32))
    return jnp.where(lane < 48, wide, 0.0)


def coarse_sweeps(coefs, source):
    x_low, x_high, y_low, y_high, z_up, scale = coefs
    start = scale * source
    c = start
    for _ in range(SWEEPS):
        beside = x_low * pltpu.roll(c, 1, 0) + x_high * pltpu.roll(c, 15, 0)
        beside = beside + y_low * pltpu.roll(c, 4, 1) + y_high * pltpu.roll(c, NZ - 4, 1)
        beside = beside + z_up * up(c) + down(z_up * c)
        c = (1.0 - W) * c + (start + scale * beside)
    return c


def spread_coarse(c, spread):
    for k in range(6):
        lane = iota((NZ, NZ), 1)
        pick = jnp.where(iota((NZ, NZ), 0) == 4 * (k + 3) + lane // 32, 1.0, 0.0)
        spread[k] = dot(c, pick.astype(F32))


def neighbours(v, fx, fy, fz, i, at, size):
    here = v[i, pl.ds(at, size), :]
    total = fx[i, pl.ds(at, size), :] * v[i - 1, pl.ds(at, size), :]
    total = total + fx[i + 1, pl.ds(at, size), :] * v[i + 1, pl.ds(at, size), :]
    total = total + fy[i, pl.ds(at, size), :] * v[i, pl.ds(at - 1, size), :]
    total = total + fy[i, pl.ds(at + 1, size), :] * v[i, pl.ds(at + 1, size), :]
    z = fz[i, pl.ds(at, size), :]
    return here, total + z * up(here) + down(z * here)


def smooth_chunk(s1, d, fx, fy, fz, scale, spread, i, at, size, j):
    here, total = neighbours(s1, fx, fy, fz, i, at, size)
    value = (2.0 - W) * here + scale[i, pl.ds(at, size), :] * total
    if spread is not None:
        value = value + spread[j + 1, pl.ds((i + 5) // 2, 1), :]
    d[i, pl.ds(at, size), :] = value


def zero_pads(v):
    def plane(i, _):
        v[i, 0:8, :] = jnp.zeros((8, NZ), F32)
        v[i, ROWS - 8 : ROWS, :] = jnp.zeros((8, NZ), F32)
        return 0

    lax.fori_loop(0, PLANES, plane, 0, unroll=True)


def looked_up(inside, table, kh, kv, i, at, size, classes, *sides):
    index = classes.astype(jnp.int32)
    values = look_up(0.5 / table[0:1, :], index)
    for side in sides:
        values = jnp.where(inside[side] > 0.5, values, OUTSIDE)
    kh[i, pl.ds(at, size), :] = values
    if 0 < i < PLANES - 1 if isinstance(i, int) else True:
        kv[i, pl.ds(at, size), :] = look_up(0.5 / table[1:2, :], index)


def set_scale(i, at, size, mask, source, fx, fy, fz, scale, centre, s1):
    rows = pl.ds(at, size)
    z = fz[i, rows, :]
    total = fx[i, rows, :] + fx[i + 1, rows, :]
    total = total + fy[i, rows, :] + fy[i, pl.ds(at + 1, size), :] + (z + down(z))
    inverse = (W * mask) * pl.reciprocal(total)
    scale[i, rows, :] = inverse
    s1[i, rows, :] = inverse * source
    if centre is not None:
        centre[i, rows, :] = total


def cells_kernel(
    inside, table, rhs, xlo, xhi, ylo, yhi, _kh, _kv, fz,
    kh, kv, fx, fy, scale, centre, s1,
):
    def rims(x, _):
        looked_up(inside, table, kh, kv, x + HX, 8, 8, ylo[x], 2)
        looked_up(inside, table, kh, kv, x + HX, 144, 8, yhi[x], 3)
        return 0

    lax.fori_loop(0, NXL, rims, 0, unroll=True)
    for n in range(3):
        for side, base, msg in ((0, 0, xlo), (1, HX + NXL, xhi)):
            looked_up(inside, table, kh, kv, base + n, OWN, NYL, msg[n], side)

    def faces(i, _):
        for at, size, j in OWN_CHUNKS:
            rows = pl.ds(at, size)
            here = kh[i, rows, :]
            fx[i, rows, :] = harmonic(kh[i - 1, rows, :], here)
            fy[i, rows, :] = harmonic(kh[i, pl.ds(at - 1, size), :], here)
        fy[i, 144:152, :] = harmonic(kh[i, 143:151, :], kh[i, 144:152, :])
        return 0

    lax.fori_loop(HX, HX + NXL, faces, 0, unroll=True)
    end = HX + NXL
    fx[end, 16:144, :] = harmonic(kh[end - 1, 16:144, :], kh[end, 16:144, :])

    def scales(x, _):
        for at, size, j in OWN_CHUNKS:
            source = rhs[x, pl.ds(at - OWN, size), :]
            set_scale(x + HX, at, size, 1.0, source, fx, fy, fz, scale, centre, s1)
        return 0

    lax.fori_loop(0, NXL, scales, 0, unroll=True)


RIM_PLANES = (1, 2, HX + NXL, HX + NXL + 1)
RIM_CHUNKS = (CHUNKS[0], CHUNKS[5])


def first_kernel(
    inside, table, xlo, xhi, ylo, yhi, left, own, right, below, above, centre,
    _kh, _kv, _fx, _fy, _fz, _scale, _s1,
    d_out, q_out, q_far, q_near, tile_out, coefs_out, kh, kv, fx, fy, fz, scale, s1,
    d, stack, spread, tiles,
):
    for n in range(3):
        for side, i in ((0, n), (1, HX + NXL + n)):
            corner = 3 * side + n
            looked_up(inside, table, kh, kv, i, 8, 8, below[corner], side, 2)
            looked_up(inside, table, kh, kv, i, 144, 8, above[corner], side, 3)

    def pads(i, _):
        ones = jnp.ones((8, NZ), F32)
        kh[i, 0:8, :] = ones
        kh[i, ROWS - 8 : ROWS, :] = ones
        fy[i, ROWS - 8 : ROWS, :] = ones
        return 0

    lax.fori_loop(0, PLANES, pads, 0, unroll=True)
    zero_pads(s1)
    zero_pads(d)

    mid = stack_tiles(stack, left, own, right)
    low = stack_tiles(stack, below[10], below[11], below[12])
    high = stack_tiles(stack, above[10], above[11], above[12])
    wide = [widen(k, low, mid, high) for k in range(6)]
    total = wide[0] + wide[1] + wide[2] + wide[3] + wide[4] + down(wide[4])
    valid = total > 0.0
    wide_scale = jnp.where(valid, W / jnp.where(valid, total, 1.0), 0.0)
    coefs = wide[:5] + [wide_scale]
    for k in range(6):
        coefs_out[k] = coefs[k]
    spread_coarse(coarse_sweeps(coefs, wide[SOURCE]), spread)

    def set_faces(i, at, size):
        rows = pl.ds(at, size)
        here = kh[i, rows, :]
        fx[i, rows, :] = harmonic(kh[i - 1, rows, :], here)
        fy[i, rows, :] = harmonic(kh[i, pl.ds(at - 1, size), :], here)
        k = kv[i, rows, :]
        z = harmonic(k, up(k))
        fz[i, rows, :] = jnp.where(iota((size, NZ), 1) < NZ - 1, z, 0.0)

    def rim_faces(i, _):
        for at, size, _j in RIM_CHUNKS:
            set_faces(i, at, size)
        return 0

    lax.fori_loop(1, PLANES - 1, rim_faces, 0, unroll=True)
    for i in RIM_PLANES:
        for at, size, _j in OWN_CHUNKS:
            set_faces(i, at, size)
    last = PLANES - 1
    for at, size, _j in CHUNKS:
        rows = pl.ds(at, size)
        fx[last, rows, :] = harmonic(kh[last - 1, rows, :], kh[last, rows, :])

    def rim_scales(i, mask, source_low, source_high):
        set_scale(i, 8, 8, mask * inside[2], source_low, fx, fy, fz, scale, None, s1)
        set_scale(i, 144, 8, mask * inside[3], source_high, fx, fy, fz, scale, None, s1)

    def own_rims(x, _):
        rim_scales(x + HX, 1.0, ylo[NXL + x], yhi[NXL + x])
        return 0

    lax.fori_loop(0, NXL, own_rims, 0, unroll=True)
    for n in range(2):
        for side, i, msg in ((0, 1 + n, xlo), (1, HX + NXL + n, xhi)):
            corner = 6 + 2 * side + n
            rim_scales(i, inside[side], below[corner], above[corner])
            for at, size, _j in OWN_CHUNKS:
                source = msg[3 + n, pl.ds(at - OWN, size), :]
                set_scale(i, at, size, inside[side], source, fx, fy, fz, scale, None, s1)

    def smooth(i, _):
        for at, size, j in CHUNKS:
            smooth_chunk(s1, d, fx, fy, fz, scale, spread, i, at, size, j)
        return 0

    lax.fori_loop(HX - 1, HX + NXL + 1, smooth, 0, unroll=True)

    def image(x, _):
        i = x + HX
        for at, size, j in OWN_CHUNKS:
            here, total = neighbours(d, fx, fy, fz, i, at, size)
            q = centre[i, pl.ds(at, size), :] * here - total
            q_out[x, pl.ds(at - OWN, size), :] = q
            d_out[x, pl.ds(at - OWN, size), :] = here
        return 0

    lax.fori_loop(0, NXL, image, 0, unroll=True)
    for a in range(4):
        for j in range(4):
            rows = pl.ds(32 * j, 32)
            source = q_out[2 * a, rows, :] + q_out[2 * a + 1, rows, :]
            tiles[pl.ds(8 * (4 * a + j), 8), :] = row_group(source)
    tiles[...] = dot(tiles[...], sum_matrix())
    tile = gather_tile(
        [
            [(SOURCE, j, tiles[pl.ds(8 * (4 * a + j), 8), :]) for j in range(4)]
            for a in range(4)
        ]
    )
    tile_out[...] = tile
    low_plane, high_plane = 0, NXL - 2
    odd = inside[4] > 0.5
    far, near = jnp.where(odd, high_plane, low_plane), jnp.where(odd, low_plane, high_plane)
    for n in range(2):
        q_far[pl.ds(128 * n, 128), :] = q_out[far + n]
        q_near[pl.ds(128 * n, 128), :] = q_out[near + n]
    q_far[256:264, :] = tile
    q_near[256:264, :] = tile


INNER_CHUNKS = ((24, 24, 0), (48, 32, 1), (80, 32, 2), (112, 24, 3))
OUTER_CHUNKS = ((8, 8, -1), (16, 8, 0), (136, 8, 3), (144, 8, 4))


def inner_kernel(rhs, d0, q0, fx, fy, fz, scale, s1, d, known):
    zero_pads(s1)
    zero_pads(d)

    def plane(x, sums):
        i = x + HX
        for at, size, j in OWN_CHUNKS:
            rows = pl.ds(at - OWN, size)
            q = q0[x, rows, :]
            s1[i, pl.ds(at, size), :] = scale[i, pl.ds(at, size), :] * q
            dd = d0[x, rows, :]
            rd, dq = sums
            sums = (rd + row_group(rhs[x, rows, :] * dd), dq + row_group(dd * q))
        return sums

    zero = jnp.zeros((8, NZ), F32)
    rd, dq = lax.fori_loop(0, NXL, plane, (zero, zero), unroll=True)
    known[0:8, :] = rd
    known[8:16, :] = dq

    def smooth(i, _):
        for at, size, j in INNER_CHUNKS:
            smooth_chunk(s1, d, fx, fy, fz, scale, None, i, at, size, j)
        return 0

    lax.fori_loop(HX + 1, HX + NXL - 1, smooth, 0, unroll=True)


def second_kernel(
    rhs, d0, q0, xlo, xhi, own, below, above, coefs, fx, fy, fz, scale, centre, known,
    _s1, _d, p_out, s_out, dots, s1, d, stack, spread,
):
    mid = stack_tiles(stack, xlo[256:264, :], own[...], xhi[256:264, :])
    low = stack_tiles(stack, below[12], below[13], below[14])
    high = stack_tiles(stack, above[12], above[13], above[14])
    wide = widen(SOURCE, low, mid, high)
    spread_coarse(coarse_sweeps([coefs[k] for k in range(6)], wide), spread)

    def rims(i, _):
        s1[i, 8:16, :] = scale[i, 8:16, :] * below[i - 1]
        s1[i, 144:152, :] = scale[i, 144:152, :] * above[i - 1]
        return 0

    lax.fori_loop(1, PLANES - 1, rims, 0, unroll=True)
    for n in range(2):
        for i, msg in ((1 + n, xlo), (HX + NXL + n, xhi)):
            s1[i, 16:144, :] = scale[i, 16:144, :] * msg[pl.ds(128 * n, 128), :]

    for i in (HX - 1, HX, HX + NXL - 1, HX + NXL):
        for at, size, j in CHUNKS:
            smooth_chunk(s1, d, fx, fy, fz, scale, spread, i, at, size, j)

    def smooth(i, _):
        for at, size, j in OUTER_CHUNKS:
            smooth_chunk(s1, d, fx, fy, fz, scale, spread, i, at, size, j)
        for at, size, j in INNER_CHUNKS:
            rows = pl.ds(at, size)
            d[i, rows, :] = d[i, rows, :] + spread[j + 1, pl.ds((i + 5) // 2, 1), :]
        return 0

    lax.fori_loop(HX + 1, HX + NXL - 1, smooth, 0, unroll=True)

    def image(x, sums):
        i = x + HX
        for at, size, j in OWN_CHUNKS:
            rows = pl.ds(at - OWN, size)
            p, total = neighbours(d, fx, fy, fz, i, at, size)
            s = centre[i, pl.ds(at, size), :] * p - total
            p_out[x, rows, :] = p
            s_out[x, rows, :] = s
            r, dd, q = rhs[x, rows, :], d0[x, rows, :], q0[x, rows, :]
            pairs = ((r, p), (q, p), (dd, s), (p, s))
            sums = tuple(
                acc + row_group(u * v) for acc, (u, v) in zip(sums, pairs)
            )
        return sums

    zero = jnp.zeros((8, NZ), F32)
    sums = lax.fori_loop(0, NXL, image, (zero,) * 4, unroll=True)
    sums = (known[0:8, :], known[8:16, :]) + sums
    sublane, lane = iota((8, NZ), 0), iota((8, NZ), 1)
    tile = zero
    for n, acc in enumerate(sums):
        tile = jnp.where(sublane == n, jnp.sum(acc, axis=0, keepdims=True), tile)
    tile = jnp.where(sublane == lane, jnp.sum(tile, axis=1, keepdims=True), 0.0)
    dots[...] = jnp.sum(tile, axis=0, keepdims=True)


def last_kernel(parts, rhs, d0, q0, p, s, x_out, r_out):
    total = parts[0:8, :]
    for n in range(8, parts.shape[0], 8):
        total = total + parts[n : n + 8, :]
    sums = jnp.sum(total, axis=0, keepdims=True)
    rd, dq, rp, qp, ds, ps = [sums[:, n : n + 1] for n in range(6)]
    a0 = rd / dq
    rz = rd - a0 * rp - a0 * dq + a0 * a0 * qp
    ratio = rz / rd
    grow = 1.0 + ratio
    curve = grow * grow * dq - grow * a0 * (ds + qp) + a0 * a0 * ps
    a1 = rz / curve
    u = jnp.broadcast_to(a0 + a1 * grow, (8, NZ))[0:1, :]
    v = jnp.broadcast_to(a1 * a0, (8, NZ))[0:1, :]

    def plane(x, _):
        for at in range(0, NYL, 32):
            rows = pl.ds(at, 32)
            x_out[x, rows, :] = u * d0[x, rows, :] - v * p[x, rows, :]
            r_out[x, rows, :] = rhs[x, rows, :] - u * q0[x, rows, :] + v * s[x, rows, :]
        return 0

    lax.fori_loop(0, NXL, plane, 0, unroll=True)


VMEM = pl.BlockSpec(memory_space=pltpu.VMEM)
SMEM = pl.BlockSpec(memory_space=pltpu.SMEM)


def call(kernel, name, operands, outs, scratch, scalars=0, aliases=None):
    return pl.pallas_call(
        kernel,
        name=name,
        out_shape=[jax.ShapeDtypeStruct(s, F32) for s in outs],
        in_specs=[SMEM] * scalars + [VMEM] * (len(operands) - scalars),
        out_specs=[VMEM] * len(outs),
        scratch_shapes=[pltpu.VMEM(s, F32) for s in scratch],
        input_output_aliases=aliases or {},
        compiler_params=pltpu.CompilerParams(vmem_limit_bytes=24 * 1024 * 1024),
    )(*operands)


def swap(values, axis, first):
    pairs = []
    for i in range(first, lax.axis_size(axis) - 1, 2):
        pairs += [(i, i + 1), (i + 1, i)]
    return lax.ppermute(values, axis, pairs)


def sides(far, near, odd):
    return jnp.where(odd, near, far), jnp.where(odd, far, near)


def swap_both(to_low, to_high, axis, odd):
    far = swap(jnp.where(odd, to_high, to_low), axis, 1)
    near = swap(jnp.where(odd, to_low, to_high), axis, 0)
    return sides(far, near, odd)


def exchange(row, axes):
    count = lax.axis_size(axes)
    rows = jnp.broadcast_to(row[None], (count, 1, NZ))
    return lax.all_to_all(rows, axes, 0, 0).reshape(count, NZ)


STAGES = (("sy", "cg"), "sx")


def body(right_side, perm_class, perm_table):
    x_at, y_at = lax.axis_index(X_AXES), lax.axis_index("sy")
    x_end, y_end = lax.axis_size(X_AXES) - 1, lax.axis_size("sy") - 1
    x_odd, y_odd = x_at % 2 == 1, y_at % 2 == 1
    flags = [x_at > 0, x_at < x_end, y_at > 0, y_at < y_end, x_odd]
    inside = jnp.stack(flags).astype(F32)
    pad = ((0, 6), (0, NZ - perm_table.shape[1]))
    table = jnp.pad(perm_table, pad, constant_values=1.0)

    def packed(classes, values):
        return jnp.concatenate([classes.astype(F32), values])

    def x_planes(low):
        classes = lax.dynamic_slice_in_dim(perm_class, jnp.where(low, 0, NXL - 3), 3)
        values = lax.dynamic_slice_in_dim(right_side, jnp.where(low, 0, NXL - 2), 2)
        return packed(classes, values)

    def y_rows(at):
        return packed(perm_class[:, at : at + 8], right_side[:, at : at + 8])

    x_far = swap(x_planes(~x_odd), X_AXES, 1)
    x_near = swap(x_planes(x_odd), X_AXES, 0)
    ylo, yhi = swap_both(y_rows(0), y_rows(NYL - 8), "sy", y_odd)
    xlo, xhi = sides(x_far, x_near, x_odd)
    block, big = (NXL, NYL, NZ), (PLANES, ROWS, NZ)
    kh, kv, fz, tiles = call(
        own_kernel, "own", (table, perm_class, right_side), [big] * 3 + [(448, NZ)], []
    )
    halos = (xlo, xhi, ylo, yhi)
    (own,) = call(
        coarse_kernel, "coarse", (inside, table) + halos + (kh, tiles), [(8, NZ)],
        [(128, NZ)], 1,
    )
    kh, kv, fx, fy, scale, centre, s1 = call(
        cells_kernel, "cells", (inside, table, right_side) + halos + (kh, kv, fz),
        [big] * 7, [], 1, {7: 0, 8: 1},
    )
    left, right = swap_both(own, own, X_AXES, x_odd)

    def rim(rows):
        parts = [xlo[:3, rows], xhi[:3, rows], xlo[3:, rows], xhi[3:, rows]]
        return jnp.concatenate(parts + [left[None], own[None], right[None]])

    below, above = swap_both(rim(slice(0, 8)), rim(slice(NYL - 8, NYL)), "sy", y_odd)

    d0, q0, q_far, q_near, tile, coefs, _, _, fx, fy, fz, scale, _ = call(
        first_kernel, "first",
        (inside, table) + halos + (left, own, right, below, above, centre)
        + (kh, kv, fx, fy, fz, scale, s1),
        [block, block, (264, NZ), (264, NZ), (8, NZ), (6, 16, NZ)] + [big] * 7,
        [big, (16, NZ), (6, 16, NZ), (16 * 8, NZ)], 1,
        {12 + n: 6 + n for n in range(7)},
    )
    qlo, qhi = sides(swap(q_far, X_AXES, 1), swap(q_near, X_AXES, 0), x_odd)
    s1, d, known = call(
        inner_kernel, "inner", (right_side, d0, q0, fx, fy, fz, scale),
        [big, big, (16, NZ)], [],
    )

    def rim_q(at):
        parts = [qlo[at : at + 8][None], qlo[128 + at : 136 + at][None], q0[:, at : at + 8]]
        parts += [qhi[at : at + 8][None], qhi[128 + at : 136 + at][None]]
        return jnp.concatenate(parts + [qlo[256:][None], tile[None], qhi[256:][None]])

    below, above = swap_both(rim_q(0), rim_q(NYL - 8), "sy", y_odd)
    p, s, dots, _, _ = call(
        second_kernel, "second",
        (right_side, d0, q0, qlo, qhi, tile, below, above, coefs, fx, fy, fz, scale, centre)
        + (known, s1, d),
        [block, block, (1, NZ), big, big], [(16, NZ), (6, 16, NZ)], 0, {15: 3, 16: 4},
    )
    for axes in STAGES[:-1]:
        dots = exchange(dots, axes).sum(0, keepdims=True)
    dots = exchange(dots, STAGES[-1])
    fast_args = (dots, right_side, d0, q0, p, s)
    total = dots.sum(0)
    rd, dq, rp, qp = total[0], total[1], total[2], total[3]
    a0 = rd / dq
    rz = rd - a0 * rp - a0 * dq + a0 * a0 * qp

    def fast():
        return tuple(call(last_kernel, "last", fast_args, [block, block], []))

    def careful():
        r1, z1, w1 = right_side - a0 * q0, d0 - a0 * p, q0 - a0 * s
        parts = jnp.stack([jnp.sum(r1 * z1), jnp.sum(z1 * w1), jnp.sum(z1 * q0)])
        left = lax.psum(parts, ("sx", "sy", "cg"))
        ratio = left[0] / rd
        a1 = left[0] / (left[1] + 2.0 * ratio * left[2] + ratio * ratio * dq)
        x = a0 * d0 + a1 * (z1 + ratio * d0)
        return x, r1 - a1 * (w1 + ratio * q0)

    return lax.cond(rz > 0.02 * rd, fast, careful)


def solution(mesh):
    cells = P(X_AXES, "sy", None)
    return jax.shard_map(
        body,
        mesh=mesh,
        in_specs=(cells, cells, P()),
        out_specs=(cells, cells),
        check_vma=False,
    )
```
